32 devices in a mesh: lat: 8 (over z, x), lon: 4 (over y, core).
Axes of the slice: x: 2, y: 2, z: 4, core: 2. Of those that a mesh axis runs over, the one named last changes fastest.
Arguments:
- state: bfloat16 [32, 32, 64, 128], P('lat', 'lon'), may hold values from -6 to 6
- obs_row: int32 [32, 32, 128], P('lat', 'lon'), may hold values from 0 to 63
- obs_count: int32 [32, 32], P('lat', 'lon'), may hold values from 0 to 128
- obs_value: float32 [32, 32, 128], P('lat', 'lon'), may hold values from -6 to 6
- obs_weight: float32 [32, 32, 128], P('lat', 'lon'), may hold values from 0.5 to 2
- quadrant: int32 [32, 32, 64], P('lat', 'lon'), may hold values from 0 to 3
- frac_lat: float32 [32, 32, 64], P('lat', 'lon'), may hold values from 0 to 1
- frac_lon: float32 [32, 32, 64], P('lat', 'lon'), may hold values from 0 to 1
- land: int32 [32, 32, 64], P('lat', 'lon'), may hold values 0 or 1
Outputs:
- analysis: bfloat16 [32, 32, 64, 128], P('lat', 'lon')
The draws below stay inside these ranges and needn't reach their ends.
All inputs are finite; a program needn't handle non-finite values. No bound on the sum of `land` on one device may be relied on, other than what follows from the above.
Results may differ from the reference program's by a relative error of at most 0.0051.
Values may be sent and summed in bfloat16 or wider, within the bound.
A program may use at most 64 MiB of HBM per device.

```python
import math
import jax
import jax.numpy as jnp
from jax import lax

M = 128
OBS = 128
RC = 64
ITERS = 6
NLAT = 32
NLON = 32


def touch_ends(values, own_key, low, largest):
    dims = values.shape
    place = [jax.random.randint(jax.random.fold_in(own_key, axis), (), 0, dims[axis]) for axis in range(len(dims))]
    values = values.at[tuple(place)].set(low)
    longest = dims.index(max(dims))
    place[longest] = (place[longest] + 1) % dims[longest]
    return values.at[tuple(place)].set(largest)


def block_levels(rng, extent, cuts, low, top_value):
    def one(position, shards_of):
        steps = jax.random.uniform(jax.random.fold_in(jax.random.fold_in(rng, 6), position), (shards_of,), jnp.float32, low / len(cuts), top_value / len(cuts))
        return jnp.repeat(jnp.exp(steps), extent[position] // shards_of).reshape((-1,) + (1,) * (len(extent) - position - 1))

    level = one(*cuts[0])
    for cut in cuts[1:]:
        level = level * one(*cut)
    return level


def gaussian(rng, shape, spread, bound, shards=(), kind=jnp.bfloat16):
    level = block_levels(rng, shape, shards, -0.22, 0.18) if shards else 1.0
    values = jax.random.normal(rng, shape, jnp.float32) * spread * level
    return jnp.minimum(jnp.maximum(values, -bound), bound).astype(kind)


def setup_inputs(seed: int = 0) -> dict:
    keys = jax.random.split(jax.random.key(seed), 10)
    return {
        "state": gaussian(keys[0], (NLAT, NLON, RC, M), 1.0, 6.0, ((0, 8), (1, 4))),
        "obs_row": touch_ends(jax.random.randint(keys[1], (NLAT, NLON, OBS), 0, RC), jax.random.fold_in(keys[1], 1), 0, RC - 1).astype(jnp.int32),
        "obs_count": touch_ends(jax.random.randint(keys[2], (NLAT, NLON), 0, OBS + 1), jax.random.fold_in(keys[2], 1), 0, OBS).astype(jnp.int32),
        "obs_value": gaussian(keys[3], (NLAT, NLON, OBS), 1.0, 6.0, ((0, 8), (1, 4)), jnp.float32),
        "obs_weight": jnp.clip(jnp.exp(math.log(2.0) - 1.3862944 * jax.random.uniform(keys[4], (NLAT, NLON, OBS), jnp.float32) ** block_levels(keys[4], (NLAT, NLON, OBS), ((0, 8), (1, 4)), -0.2, 0.2)), 0.5, 2.0),
        "quadrant": touch_ends(jax.random.randint(keys[5], (NLAT, NLON, RC), 0, 4), jax.random.fold_in(keys[5], 1), 0, 3).astype(jnp.int32),
        "frac_lat": jnp.clip(1.0 * jax.random.uniform(keys[6], (NLAT, NLON, RC), jnp.float32) ** block_levels(keys[6], (NLAT, NLON, RC), ((0, 8), (1, 4)), -0.2, 0.2), 0.0, 1.0),
        "frac_lon": jnp.clip(1.0 * jax.random.uniform(keys[7], (NLAT, NLON, RC), jnp.float32) ** block_levels(keys[7], (NLAT, NLON, RC), ((0, 8), (1, 4)), -0.2, 0.2), 0.0, 1.0),
        "land": touch_ends((jax.random.randint(keys[8], (NLAT, NLON, RC), 0, 4) < 3).astype(jnp.int32), jax.random.fold_in(keys[8], 1), 0, 1),
    }


HIGHEST = lax.Precision.HIGHEST
NEAR_WEIGHTS = (0.5, 1.0, 0.5)

def node_terms(cells, member_mean, obs_rows, counts, observed, weight):
    picked = jnp.take_along_axis(cells, obs_rows[..., None], axis=-2).astype(jnp.float32)
    centre = jnp.take_along_axis(member_mean, obs_rows, axis=-1)
    slot_ids = lax.broadcasted_iota(jnp.int32, obs_rows.shape, obs_rows.ndim - 1)
    live_weight = jnp.where(slot_ids < counts[..., None], weight, jnp.float32(0.0))
    blocks = ((picked - centre[..., None]) * live_weight[..., None]).astype(jnp.bfloat16)
    innovation = ((observed - centre) * live_weight).astype(jnp.bfloat16)
    return (blocks, innovation)

def gram_terms(blocks, innovation):
    wide_blocks = blocks.astype(jnp.float32)
    node_grams = jnp.einsum('...sm,...sn->...mn', wide_blocks, wide_blocks)
    node_sides = jnp.einsum('...sm,...s->...m', wide_blocks, innovation.astype(jnp.float32))
    return (node_grams, node_sides)

def transform_weights(gram_sum, side_sum, members):
    identity = jnp.eye(members, dtype=jnp.float32)
    frob_norm = jnp.sqrt(lax.optimization_barrier(jnp.sum(gram_sum * gram_sum, axis=(-2, -1))))
    iterate = gram_sum / frob_norm[..., None, None]
    inv_root = jnp.broadcast_to(identity, gram_sum.shape)
    for newton_step in range(ITERS):
        factor = 1.5 * identity - 0.5 * jnp.einsum('...ab,...bc->...ac', inv_root, iterate, precision=HIGHEST)
        iterate = jnp.einsum('...ab,...bc->...ac', iterate, factor, precision=HIGHEST)
        inv_root = jnp.einsum('...ab,...bc->...ac', factor, inv_root, precision=HIGHEST)
    inner_term = jnp.einsum('...ab,...b->...a', inv_root, side_sum, precision=HIGHEST)
    mean_weight = jnp.einsum('...ab,...b->...a', inv_root, inner_term, precision=HIGHEST) / frob_norm[..., None]
    spread_part = math.sqrt(members - 1) * inv_root / jnp.sqrt(frob_norm)[..., None, None]
    return (mean_weight[..., :, None] + spread_part).astype(jnp.bfloat16)

def reference(state, obs_row, obs_count, obs_value, obs_weight, quadrant, frac_lat, frac_lon, land):
    members = state.shape[3]
    row_ids = jnp.arange(NLAT, dtype=jnp.int32)

    def pick(array, row_index):
        return lax.dynamic_index_in_dim(array, row_index, 0, keepdims=False)

    def terms_row(row_index):
        cells = pick(state, row_index)
        member_mean = lax.optimization_barrier(jnp.mean(cells.astype(jnp.float32), axis=-1))
        return node_terms(cells, member_mean, pick(obs_row, row_index), pick(obs_count, row_index), pick(obs_value, row_index), pick(obs_weight, row_index))
    blocks, innovation = lax.map(terms_row, row_ids)
    padded_blocks = jnp.pad(blocks, ((1, 1), (0, 0), (0, 0), (0, 0)))
    padded_innov = jnp.pad(innovation, ((1, 1), (0, 0), (0, 0)))

    def weight_row(row_index):
        near_blocks = lax.dynamic_slice_in_dim(padded_blocks, row_index, 3, 0)
        near_innov = lax.dynamic_slice_in_dim(padded_innov, row_index, 3, 0)
        node_grams, node_sides = gram_terms(near_blocks, near_innov)
        identity = jnp.eye(members, dtype=jnp.float32)
        gram_sum = jnp.zeros((NLON, members, members), jnp.float32) + (members - 1) * identity
        side_sum = jnp.zeros((NLON, members), jnp.float32)
        for lat_off in range(3):
            for lon_off in range(3):
                factor = NEAR_WEIGHTS[lat_off] * NEAR_WEIGHTS[lon_off]
                gram_sum = gram_sum + factor * jnp.roll(node_grams[lat_off], 1 - lon_off, axis=0)
                side_sum = side_sum + factor * jnp.roll(node_sides[lat_off], 1 - lon_off, axis=0)
        return transform_weights(gram_sum, side_sum, members)
    weights = lax.map(weight_row, row_ids)
    padded_weights = jnp.pad(weights, ((1, 1), (0, 0), (0, 0), (0, 0)))

    def analysis_row(row_index):
        near_weights = lax.dynamic_slice_in_dim(padded_weights, row_index, 3, 0)
        cells = pick(state, row_index)
        values = cells.astype(jnp.float32)
        member_mean = lax.optimization_barrier(jnp.mean(values, axis=-1))
        perturb = (values - member_mean[..., None]).astype(jnp.bfloat16)
        corner_ids = pick(quadrant, row_index)
        lat_half = corner_ids // 2
        lon_half = corner_ids % 2
        lat_frac = pick(frac_lat, row_index)
        lon_frac = pick(frac_lon, row_index)
        accumulated = jnp.zeros(values.shape, jnp.float32)
        for lat_off in range(3):
            along_lat = jnp.where(lat_half == lat_off, 1.0 - lat_frac, 0.0) + jnp.where(lat_half + 1 == lat_off, lat_frac, 0.0)
            for lon_off in range(3):
                along_lon = jnp.where(lon_half == lon_off, 1.0 - lon_frac, 0.0) + jnp.where(lon_half + 1 == lon_off, lon_frac, 0.0)
                shifted = jnp.roll(near_weights[lat_off], 1 - lon_off, axis=0)
                product = jnp.einsum('jrm,jmn->jrn', perturb.astype(jnp.float32), shifted.astype(jnp.float32))
                accumulated = accumulated + (along_lat * along_lon)[..., None] * product
        land_row = pick(land, row_index)
        result = jnp.where(land_row[..., None] == 1, member_mean[..., None] + accumulated, values)
        return result.astype(jnp.bfloat16)
    return lax.map(analysis_row, row_ids)
```

```python
import functools
import math

import jax
import jax.numpy as jnp
from jax import lax
from jax.experimental import pallas as pl
from jax.experimental.pallas import tpu as pltpu
from jax.sharding import PartitionSpec as P

ITERS = 6
NEAR = (0.5, 1.0, 0.5)
SIDE_ROWS = 8
F32 = jnp.float32
BF16 = jnp.bfloat16
MESH = pl.DeviceIdType.MESH
WAYS = ((-1, 0), (1, 0), (0, -1), (0, 1))
CORNERS = ((-1, -1), (-1, 1), (1, -1), (1, 1))


def nn(a, b):
    return lax.dot_general(a, b, (((1,), (0,)), ((), ())), preferred_element_type=F32)


def nt(a, b):
    return lax.dot_general(a, b, (((1,), (1,)), ((), ())), preferred_element_type=F32)


def tn(a, b):
    return lax.dot_general(a, b, (((0,), (0,)), ((), ())), preferred_element_type=F32)


def group_of(count, most=4):
    return next(g for g in range(most, 0, -1) if count % g == 0)


def prep_kernel(count_ref, state_ref, row_ref, value_ref, weight_ref, out_ref):
    tile_lat, tile_lon, cells, members = state_ref.shape
    slots = row_ref.shape[-1]
    nodes = tile_lat * tile_lon
    group = group_of(nodes, 8)

    def step(t, carry):
        for g in range(group):
            node = t * group + g
            i, j = node // tile_lon, node % tile_lon
            values = state_ref[i, j].astype(F32)
            mean = jnp.sum(values, axis=1, keepdims=True) * (1.0 / members)
            pert = values - mean
            lane = lax.broadcasted_iota(jnp.int32, (1, slots), 1)
            weight = jnp.where(lane < count_ref[i, j], weight_ref[i, pl.ds(j, 1), :], 0.0)
            square = weight * weight
            hit = row_ref[i, pl.ds(j, 1), :] == lax.broadcasted_iota(jnp.int32, (cells, slots), 0)
            density = jnp.sum(jnp.where(hit, square, 0.0), axis=1, keepdims=True)
            pulled = jnp.sum(
                jnp.where(hit, square * value_ref[i, pl.ds(j, 1), :], 0.0), axis=1, keepdims=True
            )
            out_ref[i, j, pl.ds(0, cells), :] = (jnp.sqrt(density) * pert).astype(BF16)
            side = jnp.sum(pert * (pulled - density * mean), axis=0, keepdims=True)
            high = side.astype(BF16).astype(F32)
            which = lax.broadcasted_iota(jnp.int32, (SIDE_ROWS, members), 0)
            tail = jnp.where(which == 0, high, jnp.where(which == 1, side - high, 0.0))
            out_ref[i, j, pl.ds(cells, SIDE_ROWS), :] = tail.astype(BF16)
        return carry

    lax.fori_loop(0, nodes // group, step, 0)


def edge_slices(step, size):
    if step == 0:
        return slice(0, size), slice(1, size + 1), size
    if step < 0:
        return 0, size + 1, 1
    return size - 1, 0, 1


def main_kernel(
    counts, qx_ref, state_ref, quadrant_ref, frac_lat_ref, frac_lon_ref, land_ref,
    out_ref, qbuf, wbuf, q_send, q_recv, w_send, w_recv, r_send, r_recv,
    c_send, c_recv,
):
    n_lat, n_lon = counts
    row_parts = r_send.shape[1]
    tile_lat, tile_lon, cells, members = state_ref.shape
    lat, lon = lax.axis_index("lat"), lax.axis_index("lon")

    def exists(way):
        if way[0] < 0:
            return lat > 0
        if way[0] > 0:
            return lat < n_lat - 1
        return None

    def where_exists(way, do):
        if way[0] == 0:
            do()
        else:
            pl.when(exists(way))(do)

    def peer(way):
        return (lat + way[0], lax.rem(lon + way[1] + n_lon, n_lon))

    def at(ref, i, j):
        i = pl.ds(i.start, i.stop - i.start) if isinstance(i, slice) else i
        j = pl.ds(j.start, j.stop - j.start) if isinstance(j, slice) else j
        return ref.at[i, j]

    def copy(source, offset, buffer, send, recv, index):
        way = WAYS[index]
        si, di, _ = edge_slices(way[0], tile_lat)
        sj, dj, _ = edge_slices(way[1], tile_lon)

        def moved(s):
            return slice(s.start + offset, s.stop + offset) if isinstance(s, slice) else s + offset

        return pltpu.make_async_remote_copy(
            src_ref=at(source, moved(si), moved(sj)),
            dst_ref=at(buffer, di, dj),
            send_sem=send.at[index],
            recv_sem=recv.at[index],
            device_id=peer(way),
            device_id_type=MESH,
        )

    def q_copy(index):
        return copy(qx_ref, 0, qbuf, q_send, q_recv, index)

    def w_copy(index):
        return copy(wbuf, 1, wbuf, w_send, w_recv, index)

    def row_copy(index, part):
        source, target, _ = edge_slices(WAYS[index][0], tile_lat)
        width = tile_lon // row_parts
        columns = pl.ds(1 + part * width, width)
        return pltpu.make_async_remote_copy(
            src_ref=wbuf.at[source + 1, columns],
            dst_ref=wbuf.at[target, columns],
            send_sem=r_send.at[index, part],
            recv_sem=r_recv.at[index, part],
            device_id=peer(WAYS[index]),
            device_id_type=MESH,
        )

    def corner_copy(buffer, stage, index):
        side, step = CORNERS[index]
        row = 0 if side < 0 else tile_lat + 1
        source, target = (1, tile_lon + 1) if step < 0 else (tile_lon, 0)
        return pltpu.make_async_remote_copy(
            src_ref=buffer.at[row, source],
            dst_ref=buffer.at[row, target],
            send_sem=c_send.at[stage, index],
            recv_sem=c_recv.at[stage, index],
            device_id=peer((0, step)),
            device_id_type=MESH,
        )

    def each_corner(buffer, stage, do):
        for index, way in enumerate(CORNERS):
            where_exists(way, lambda index=index: do(corner_copy(buffer, stage, index)))

    barrier = pltpu.get_barrier_semaphore()
    for way in WAYS:
        where_exists(way, lambda way=way: pl.semaphore_signal(
            barrier, inc=1, device_id=peer(way), device_id_type=MESH))
    present = 2 + (lat > 0).astype(jnp.int32) + (lat < n_lat - 1).astype(jnp.int32)
    pl.semaphore_wait(barrier, present)
    for index, way in enumerate(WAYS):
        where_exists(way, lambda index=index: q_copy(index).start())

    @pl.when(lat == 0)
    def _():
        qbuf[0] = jnp.zeros(qbuf.shape[1:], BF16)
        wbuf[0] = jnp.zeros(wbuf.shape[1:], BF16)

    @pl.when(lat == n_lat - 1)
    def _():
        qbuf[tile_lat + 1] = jnp.zeros(qbuf.shape[1:], BF16)
        wbuf[tile_lat + 1] = jnp.zeros(wbuf.shape[1:], BF16)

    for i in range(tile_lat):
        qbuf[i + 1, pl.ds(1, tile_lon)] = qx_ref[i]

    def received(index, make):
        way = WAYS[index]
        back = (-way[0], -way[1])
        where_exists(back, lambda: make(index).wait_recv())

    def sent(index, make):
        where_exists(WAYS[index], lambda: make(index).wait_send())

    eye = (
        lax.broadcasted_iota(jnp.int32, (members, members), 0)
        == lax.broadcasted_iota(jnp.int32, (members, members), 1)
    ).astype(F32)
    eye_b = eye.astype(BF16)

    def gram_of(i, j):
        left, right = [], []
        tail = jnp.zeros((SIDE_ROWS, members), F32)
        for b in range(3):
            for a in range(3):
                scale = NEAR[a] * NEAR[b]
                block = qbuf[i + a, j + b, pl.ds(0, cells), :]
                right.append(block)
                left.append(block if scale == 1.0 else block * jnp.asarray(scale, BF16))
                tail += scale * qbuf[i + a, j + b, pl.ds(cells, SIDE_ROWS), :].astype(F32)
        gram = tn(jnp.concatenate(left, axis=0), jnp.concatenate(right, axis=0))
        return gram, jnp.sum(tail, axis=0, keepdims=True)

    def total(x):
        return jnp.sum(jnp.sum(x, axis=0, keepdims=True), axis=1, keepdims=True)

    def pair_factor(scale):
        first = 1.5 - 0.5 * scale
        r = 0.5 * scale / first
        middle = scale * first * first
        second = 1.5 - 0.5 * middle
        q = 0.5 * middle / second
        p1, p2, p3 = 1.0 - 2.0 * r, r * r - 2.0 * r, r * r
        coefs = (-r - q * p1, q * (r * p1 - p2), q * (r * p2 - p3), q * r * p3)
        both = first * second
        return both, coefs, scale * both * both

    def transform(places):
        group = range(len(places))
        xs, sides, scalars = [], [], []
        for i, j in places:
            gram, side = gram_of(i, j)
            ridge = members - 1.0
            trace = total(gram * eye)
            frob = jnp.sqrt(total(gram * gram) + 2.0 * ridge * trace + ridge * ridge * members)
            centre = ridge + trace * (1.0 / members)
            inv = 1.0 / centre
            xs.append(gram * inv + eye * (ridge * inv - 1.0))
            sides.append(side)
            scale = centre / frob
            root, steps = 1.0, []
            for _ in range(ITERS // 2):
                both, coefs, scale = pair_factor(scale)
                root = root * both
                steps.append(coefs)
            scalars.append((frob, root, steps))
        zs = [None for _ in group]
        for step in range(ITERS // 2):
            last = step == ITERS // 2 - 1
            squares, ds, gs = [], [], []
            for x in xs:
                xb = x.astype(BF16)
                squares.append(nn(xb, xb))
            for n in group:
                a1, a2, a3, a4 = scalars[n][2][step]
                x, s = xs[n], squares[n]
                tail = nn(s.astype(BF16), (a3 * x + a4 * s).astype(BF16))
                ds.append(a1 * x + a2 * s + tail)
            for n in group:
                d = ds[n]
                db = d.astype(BF16)
                if not last:
                    gs.append((xs[n] + d) + nn(db, xs[n].astype(BF16)))
                zs[n] = d if step == 0 else (zs[n] + d) + nn(db, zs[n].astype(BF16))
            if not last:
                xs = [(gs[n] + ds[n]) + nn(ds[n].astype(BF16), gs[n].astype(BF16)) for n in group]
        which = lax.broadcasted_iota(jnp.int32, (SIDE_ROWS, members), 0)
        for n, (i, j) in enumerate(places):
            frob, root, _ = scalars[n]
            side = sides[n]
            zb = zs[n].astype(BF16)
            high = side.astype(BF16).astype(F32)
            rows = jnp.where(which == 0, high, jnp.where(which == 1, side - high, 0.0))
            inner = side + jnp.sum(nn(rows.astype(BF16), zb), axis=0, keepdims=True)
            inner = inner * (root * root / frob)
            high = inner.astype(BF16)
            low = (inner - high.astype(F32)).astype(BF16)
            high = jnp.broadcast_to(high, (members, members))
            low = jnp.broadcast_to(low, (members, members))
            mean_weight = nt(
                jnp.concatenate([zb, eye_b, eye_b], axis=1),
                jnp.concatenate([high, high, low], axis=1),
            )
            spread = math.sqrt(members - 1) * root / jnp.sqrt(frob)
            wbuf[i + 1, j + 1] = (mean_weight + spread * (zs[n] + eye)).astype(BF16)

    mid_lat, mid_lon = tile_lat - 2, tile_lon - 2
    n_rows, n_sides, n_inner = 2 * tile_lon, 2 * mid_lat, mid_lat * mid_lon
    group = next(g for g in (4, 2) if all(n % g == 0 for n in (n_rows, n_sides, n_inner)))
    g_rows, g_sides, g_inner = n_rows // group, n_sides // group, n_inner // group
    wide = next(g for g in range(16, 0, -1) if n_rows % g == 0 and mid_lat * tile_lon % g == 0)
    w_rows, w_rest = n_rows // wide, mid_lat * tile_lon // wide

    def row_place(k):
        return (k % 2) * (tile_lat - 1), k // 2

    def side_place(k):
        return 1 + k // 2, (k % 2) * (tile_lon - 1)

    def inner_place(k):
        return 1 + k // mid_lon, 1 + k % mid_lon

    def place(slot, g):
        row = row_place(jnp.minimum(slot, w_rows - 1) * wide + g)
        k = jnp.maximum(slot - w_rows, 0) * wide + g
        rest = 1 + k // tile_lon, k % tile_lon
        is_row = slot < w_rows
        return jnp.where(is_row, row[0], rest[0]), jnp.where(is_row, row[1], rest[1])

    for index in range(2):
        received(index, q_copy)
    each_corner(qbuf, 0, lambda copy: copy.start())
    for index in range(2, 4):
        received(index, q_copy)
    each_corner(qbuf, 0, lambda copy: copy.wait_recv())

    def node_step(slot, carry):
        transform([place(slot, g) for g in range(wide)])

        for index in range(2):
            pl.when(exists(WAYS[index]) & (slot == w_rows - 1))(
                lambda index=index: row_copy(index, 0).start())
        return carry

    lax.fori_loop(0, w_rows + w_rest, node_step, 0)
    for index in range(2, 4):
        w_copy(index).start()

    def analyse(i, j):
        values = state_ref[i, j].astype(F32)
        mean = jnp.sum(values, axis=1, keepdims=True) * (1.0 / members)
        pert = (values - mean).astype(BF16)
        corner = quadrant_ref[i, pl.ds(j, 1), :]
        along = []
        for half, frac in (
            (corner // 2, frac_lat_ref[i, pl.ds(j, 1), :]),
            (corner % 2, frac_lon_ref[i, pl.ds(j, 1), :]),
        ):
            for a in range(3):
                along.append(
                    jnp.where(half == a, 1.0 - frac, 0.0) + jnp.where(half + 1 == a, frac, 0.0)
                )
        along.append(land_ref[i, pl.ds(j, 1), :].astype(F32))
        along.append(jnp.zeros_like(along[0]))
        coef = jnp.transpose(jnp.concatenate(along, axis=0))
        acc = mean
        for a in range(3):
            wide = jnp.concatenate([wbuf[i + a, j + b] for b in range(3)], axis=1)
            prod = nn(pert, wide)
            row = sum(
                coef[:, 3 + b : 4 + b] * prod[:, b * members : (b + 1) * members] for b in range(3)
            )
            acc = acc + coef[:, a : a + 1] * row
        result = jnp.where(coef[:, 6:7] == 1.0, acc, values)
        out_ref[i, j] = result.astype(BF16)

    def inner_step(t, carry):
        for g in range(group):
            analyse(*inner_place(t * group + g))
        return carry

    lax.fori_loop(0, g_inner, inner_step, 0)
    for index in range(2):
        for part in range(row_parts):
            received(index, lambda index, part=part: row_copy(index, part))
    each_corner(wbuf, 1, lambda copy: copy.start())
    for index in range(2, len(WAYS)):
        received(index, w_copy)

    def rim_step(t, carry):
        @pl.when(t == g_sides + g_rows - 2)
        def _():
            each_corner(wbuf, 1, lambda copy: copy.wait_recv())

        part = lax.rem(t - g_sides + 1 + g_rows, g_rows)
        first = jnp.where(t < g_sides, n_rows + t * group, part * group)
        for g in range(group):
            k = first + g
            row, side = row_place(jnp.minimum(k, n_rows - 1)), side_place(jnp.maximum(k - n_rows, 0))
            analyse(jnp.where(k < n_rows, row[0], side[0]), jnp.where(k < n_rows, row[1], side[1]))
        return carry

    lax.fori_loop(0, g_rows + g_sides, rim_step, 0)
    for index in range(len(WAYS)):
        sent(index, q_copy)
        if index >= 2:
            sent(index, w_copy)
        else:
            for part in range(row_parts):
                sent(index, lambda index, part=part: row_copy(index, part))
    each_corner(qbuf, 0, lambda copy: copy.wait_send())
    each_corner(wbuf, 1, lambda copy: copy.wait_send())


VM = pl.BlockSpec(memory_space=pltpu.VMEM)


def body(counts, state, obs_row, obs_count, obs_value, obs_weight, quadrant, frac_lat, frac_lon, land):
    tile_lat, tile_lon, cells, members = state.shape
    rows = cells + SIDE_ROWS
    row_parts = 1
    qx = pl.pallas_call(
        prep_kernel,
        out_shape=jax.ShapeDtypeStruct((tile_lat, tile_lon, rows, members), BF16),
        in_specs=[pl.BlockSpec(memory_space=pltpu.SMEM)] + [VM] * 4,
        out_specs=VM,
        name="prep",
    )(obs_count, state, obs_row, obs_value, obs_weight)
    return pl.pallas_call(
        functools.partial(main_kernel, counts),
        out_shape=jax.ShapeDtypeStruct(state.shape, BF16),
        in_specs=[VM] * 6,
        out_specs=VM,
        scratch_shapes=[
            pltpu.VMEM((tile_lat + 2, tile_lon + 2, rows, members), BF16),
            pltpu.VMEM((tile_lat + 2, tile_lon + 2, members, members), BF16),
            pltpu.SemaphoreType.DMA((4,)),
            pltpu.SemaphoreType.DMA((4,)),
            pltpu.SemaphoreType.DMA((4,)),
            pltpu.SemaphoreType.DMA((4,)),
            pltpu.SemaphoreType.DMA((2, row_parts)),
            pltpu.SemaphoreType.DMA((2, row_parts)),
            pltpu.SemaphoreType.DMA((2, 4)),
            pltpu.SemaphoreType.DMA((2, 4)),
        ],
        compiler_params=pltpu.CompilerParams(
            collective_id=0, has_side_effects=True, vmem_limit_bytes=48 * 1024 * 1024
        ),
        name="analyse",
    )(qx, state, quadrant, frac_lat, frac_lon, land)


def solution(mesh):
    counts = (mesh.shape["lat"], mesh.shape["lon"])
    return jax.shard_map(
        functools.partial(body, counts),
        mesh=mesh,
        in_specs=(
            P("lat", "lon", None, None),
            P("lat", "lon", None),
            P("lat", "lon"),
            P("lat", "lon", None),
            P("lat", "lon", None),
            P("lat", "lon", None),
            P("lat", "lon", None),
            P("lat", "lon", None),
            P("lat", "lon", None),
        ),
        out_specs=P("lat", "lon", None, None),
        check_vma=False,
    )
```

```python
import functools
import math

import jax
import jax.numpy as jnp
from jax import lax
from jax.experimental import pallas as pl
from jax.experimental.pallas import tpu as pltpu
from jax.sharding import PartitionSpec as P

ITERS = 6
NEAR = (0.5, 1.0, 0.5)
SIDE_ROWS = 8
F32 = jnp.float32
BF16 = jnp.bfloat16
MESH = pl.DeviceIdType.MESH
WAYS = ((-1, 0), (1, 0), (0, -1), (0, 1))
CORNERS = ((-1, -1), (-1, 1), (1, -1), (1, 1))


def nn(a, b):
    return lax.dot_general(a, b, (((1,), (0,)), ((), ())), preferred_element_type=F32)


def nt(a, b):
    return lax.dot_general(a, b, (((1,), (1,)), ((), ())), preferred_element_type=F32)


def tn(a, b):
    return lax.dot_general(a, b, (((0,), (0,)), ((), ())), preferred_element_type=F32)


def group_of(count, most=4):
    return next(g for g in range(most, 0, -1) if count % g == 0)


def prep_kernel(count_ref, state_ref, row_ref, value_ref, weight_ref, out_ref):
    tile_lat, tile_lon, cells, members = state_ref.shape
    slots = row_ref.shape[-1]
    nodes = tile_lat * tile_lon
    group = group_of(nodes, 8)

    def step(t, carry):
        for g in range(group):
            node = t * group + g
            i, j = node // tile_lon, node % tile_lon
            values = state_ref[i, j].astype(F32)
            mean = jnp.sum(values, axis=1, keepdims=True) * (1.0 / members)
            pert = values - mean
            lane = lax.broadcasted_iota(jnp.int32, (1, slots), 1)
            weight = jnp.where(lane < count_ref[i, j], weight_ref[i, pl.ds(j, 1), :], 0.0)
            square = weight * weight
            hit = row_ref[i, pl.ds(j, 1), :] == lax.broadcasted_iota(jnp.int32, (cells, slots), 0)
            density = jnp.sum(jnp.where(hit, square, 0.0), axis=1, keepdims=True)
            pulled = jnp.sum(
                jnp.where(hit, square * value_ref[i, pl.ds(j, 1), :], 0.0), axis=1, keepdims=True
            )
            out_ref[i, j, pl.ds(0, cells), :] = (jnp.sqrt(density) * pert).astype(BF16)
            side = jnp.sum(pert * (pulled - density * mean), axis=0, keepdims=True)
            high = side.astype(BF16).astype(F32)
            which = lax.broadcasted_iota(jnp.int32, (SIDE_ROWS, members), 0)
            tail = jnp.where(which == 0, high, jnp.where(which == 1, side - high, 0.0))
            out_ref[i, j, pl.ds(cells, SIDE_ROWS), :] = tail.astype(BF16)
        return carry

    lax.fori_loop(0, nodes // group, step, 0)


def edge_slices(step, size):
    if step == 0:
        return slice(0, size), slice(1, size + 1), size
    if step < 0:
        return 0, size + 1, 1
    return size - 1, 0, 1


def main_kernel(
    counts, qx_ref, state_ref, quadrant_ref, frac_lat_ref, frac_lon_ref, land_ref,
    out_ref, qbuf, wbuf, wpack, whalo, q_send, q_recv, w_send, w_recv, r_send, r_recv,
    c_send, c_recv,
):
    n_lat, n_lon = counts
    row_parts = r_send.shape[1]
    tile_lat, tile_lon, cells, members = state_ref.shape
    lat, lon = lax.axis_index("lat"), lax.axis_index("lon")

    def exists(way):
        if way[0] < 0:
            return lat > 0
        if way[0] > 0:
            return lat < n_lat - 1
        return None

    def where_exists(way, do):
        if way[0] == 0:
            do()
        else:
            pl.when(exists(way))(do)

    def peer(way):
        return (lat + way[0], lax.rem(lon + way[1] + n_lon, n_lon))

    def at(ref, i, j):
        i = pl.ds(i.start, i.stop - i.start) if isinstance(i, slice) else i
        j = pl.ds(j.start, j.stop - j.start) if isinstance(j, slice) else j
        return ref.at[i, j]

    def remote(source, target, way, send, recv):
        return pltpu.make_async_remote_copy(
            src_ref=source,
            dst_ref=target,
            send_sem=send,
            recv_sem=recv,
            device_id=peer(way),
            device_id_type=MESH,
        )

    def q_copy(index):
        way = WAYS[index]
        si, di, _ = edge_slices(way[0], tile_lat)
        sj, dj, _ = edge_slices(way[1], tile_lon)
        return remote(
            at(qx_ref, si, sj), at(qbuf, di, dj), way, q_send.at[index], q_recv.at[index]
        )

    def w_copy(index, part):
        way = WAYS[2 + index]
        source, target = (1, tile_lon + 1) if way[1] < 0 else (tile_lon, 0)
        rows = (pl.ds(2, tile_lat - 2), pl.ds(1, 1), pl.ds(tile_lat, 1))[part]
        return remote(
            wbuf.at[rows, source], wbuf.at[rows, target], way,
            w_send.at[index, part], w_recv.at[index, part],
        )

    def row_copy(index, part):
        width = tile_lon // row_parts
        return remote(
            wpack.at[index, pl.ds(part * width, width)],
            whalo.at[1 - index, pl.ds(1 + part * width, width)],
            WAYS[index], r_send.at[index, part], r_recv.at[index, part],
        )

    def corner_copy(stage, index):
        side, step = CORNERS[index]
        source, target = (1, tile_lon + 1) if step < 0 else (tile_lon, 0)
        buffer, row = (qbuf, 0 if side < 0 else tile_lat + 1) if stage == 0 else (whalo, (side + 1) // 2)
        return remote(
            buffer.at[row, source], buffer.at[row, target], (0, step),
            c_send.at[stage, index], c_recv.at[stage, index],
        )

    def each_corner(stage, do):
        for index, way in enumerate(CORNERS):
            where_exists(way, lambda index=index: do(corner_copy(stage, index)))

    barrier = pltpu.get_barrier_semaphore()
    for way in WAYS:
        where_exists(way, lambda way=way: pl.semaphore_signal(
            barrier, inc=1, device_id=peer(way), device_id_type=MESH))
    present = 2 + (lat > 0).astype(jnp.int32) + (lat < n_lat - 1).astype(jnp.int32)
    pl.semaphore_wait(barrier, present)
    for index, way in enumerate(WAYS):
        where_exists(way, lambda index=index: q_copy(index).start())

    @pl.when(lat == 0)
    def _():
        qbuf[0] = jnp.zeros(qbuf.shape[1:], BF16)
        whalo[0] = jnp.zeros(whalo.shape[1:], BF16)

    @pl.when(lat == n_lat - 1)
    def _():
        qbuf[tile_lat + 1] = jnp.zeros(qbuf.shape[1:], BF16)
        whalo[1] = jnp.zeros(whalo.shape[1:], BF16)

    for i in range(tile_lat):
        qbuf[i + 1, pl.ds(1, tile_lon)] = qx_ref[i]

    def received(index, make):
        way = WAYS[index]
        back = (-way[0], -way[1])
        where_exists(back, lambda: make(index).wait_recv())

    def sent(index, make):
        where_exists(WAYS[index], lambda: make(index).wait_send())

    eye = (
        lax.broadcasted_iota(jnp.int32, (members, members), 0)
        == lax.broadcasted_iota(jnp.int32, (members, members), 1)
    ).astype(F32)

    which = lax.broadcasted_iota(jnp.int32, (SIDE_ROWS, members), 0)
    line = lax.broadcasted_iota(jnp.int32, (members // 2, members), 0)
    lane = lax.broadcasted_iota(jnp.int32, (members // 2, members), 1)
    upper = lane >= line

    def through(row, matrix):
        high = row.astype(BF16).astype(F32)
        rows = jnp.where(which == 0, high, jnp.where(which == 1, row - high, 0.0))
        return jnp.sum(nn(rows.astype(BF16), matrix), axis=0, keepdims=True)

    def column(row):
        return jnp.transpose(jnp.broadcast_to(row, (members, members)))

    def gram_of(i, j):
        left, right = [], []
        tail = jnp.zeros((SIDE_ROWS, members), F32)
        for b in range(3):
            for a in range(3):
                scale = NEAR[a] * NEAR[b]
                block = qbuf[i + a, j + b, pl.ds(0, cells), :]
                right.append(block)
                left.append(block if scale == 1.0 else block * jnp.asarray(scale, BF16))
                tail += scale * qbuf[i + a, j + b, pl.ds(cells, SIDE_ROWS), :].astype(F32)
        gram = tn(jnp.concatenate(left, axis=0), jnp.concatenate(right, axis=0))
        return gram, jnp.sum(tail, axis=0, keepdims=True)

    def total(x):
        return jnp.sum(jnp.sum(x, axis=0, keepdims=True), axis=1, keepdims=True)

    def pair_factor(scale):
        first = 1.5 - 0.5 * scale
        r = 0.5 * scale / first
        middle = scale * first * first
        second = 1.5 - 0.5 * middle
        q = 0.5 * middle / second
        p1, p2, p3 = 1.0 - 2.0 * r, r * r - 2.0 * r, r * r
        coefs = (-r - q * p1, q * (r * p1 - p2), q * (r * p2 - p3), q * r * p3)
        both = first * second
        return both, coefs, scale * both * both

    def transform(places, pack_at=None):
        pack = pack_at is not None
        group = range(len(places))
        xs, sides, scalars = [], [], []
        for i, j in places:
            gram, side = gram_of(i, j)
            ridge = members - 1.0
            trace = total(gram * eye)
            frob = jnp.sqrt(total(gram * gram) + 2.0 * ridge * trace + ridge * ridge * members)
            centre = ridge + trace * (1.0 / members)
            inv = 1.0 / centre
            xs.append(gram * inv + eye * (ridge * inv - 1.0))
            sides.append(side)
            scale = centre / frob
            root, steps = 1.0, []
            for _ in range(ITERS // 2):
                both, coefs, scale = pair_factor(scale)
                root = root * both
                steps.append(coefs)
            scalars.append((frob, root, steps))
        zs = [None for _ in group]
        for step in range(ITERS // 2):
            last = step == ITERS // 2 - 1
            squares, ds, gs = [], [], []
            for x in xs:
                xb = x.astype(BF16)
                squares.append(nn(xb, xb))
            for n in group:
                a1, a2, a3, a4 = scalars[n][2][step]
                x, s = xs[n], squares[n]
                tail = nn(s.astype(BF16), (a3 * x + a4 * s).astype(BF16))
                ds.append(a1 * x + a2 * s + tail)
            for n in group:
                d = ds[n]
                db = d.astype(BF16)
                if not last:
                    gs.append((xs[n] + d) + nn(db, xs[n].astype(BF16)))
                zs[n] = d if step == 0 else (zs[n] + d) + nn(db, zs[n].astype(BF16))
            if not last:
                xs = [(gs[n] + ds[n]) + nn(ds[n].astype(BF16), gs[n].astype(BF16)) for n in group]
        for n, (i, j) in enumerate(places):
            frob, root, _ = scalars[n]
            zb = zs[n].astype(BF16)
            inner = sides[n] + through(sides[n], zb)
            inner = inner * (root * root / frob)
            mean_weight = inner + through(inner, zb)
            spread = math.sqrt(members - 1) * root / jnp.sqrt(frob)
            part = spread * (zs[n] + eye)
            wbuf[i + 1, j + 1] = (part + column(mean_weight)).astype(BF16)
            if pack:
                half = members // 2
                swapped = jnp.concatenate([part[half:, half:], part[half:, :half]], axis=1)
                wpack[pack_at(n)[0], pack_at(n)[1], pl.ds(0, half), :] = jnp.where(
                    upper, part[:half], swapped
                ).astype(BF16)
                diagonal = jnp.sum(part * eye, axis=0, keepdims=True)
                high = mean_weight.astype(BF16).astype(F32)
                wpack[pack_at(n)[0], pack_at(n)[1], pl.ds(half, SIDE_ROWS), :] = jnp.where(
                    which == 0, diagonal,
                    jnp.where(which == 1, high, jnp.where(which == 2, mean_weight - high, 0.0)),
                ).astype(BF16)

    def unpack(side, j):
        half = members // 2
        sent = whalo[side, j, pl.ds(0, half), :]
        tail = whalo[side, j, pl.ds(half, SIDE_ROWS), :].astype(F32)
        turned = jnp.transpose(jnp.concatenate([sent, sent], axis=0)).astype(F32)
        sent = sent.astype(F32)
        swapped = jnp.concatenate([sent[:, half:], sent[:, :half]], axis=1)
        top = jnp.where(upper, sent, turned[:half])
        low = jnp.where(lane >= half, jnp.where(lane - half < line, swapped, turned[:half]), turned[half:])
        low = jnp.where(lane - half == line, tail[0:1], low)
        whole = jnp.concatenate([top, low], axis=0) + column(tail[1:2] + tail[2:3])
        wbuf[side * (tile_lat + 1), j] = whole.astype(BF16)

    mid_lat, mid_lon = tile_lat - 2, tile_lon - 2
    n_rows, n_sides, n_inner = 2 * tile_lon, 2 * mid_lat, mid_lat * mid_lon
    group = next(g for g in (4, 2) if all(n % g == 0 for n in (n_rows, n_sides, n_inner)))
    g_rows, g_sides, g_inner = n_rows // group, n_sides // group, n_inner // group
    wide = next(g for g in range(16, 0, -1) if mid_lat * tile_lon % g == 0)
    part_lon = tile_lon // row_parts
    w_rest = mid_lat * tile_lon // wide

    def row_place(k):
        return (k % 2) * (tile_lat - 1), k // 2

    def side_place(k):
        return 1 + k // 2, (k % 2) * (tile_lon - 1)

    def inner_place(k):
        return 1 + k // mid_lon, 1 + k % mid_lon

    for index in range(2, 4):
        received(index, q_copy)

    def rest_step(slot, carry):
        ks = [slot * wide + g for g in range(wide)]
        transform([(1 + k // tile_lon, k % tile_lon) for k in ks])
        return carry

    lax.fori_loop(0, w_rest, rest_step, 0)
    for index in range(2):
        w_copy(index, 0).start()
    for index in range(2):
        received(index, q_copy)
    each_corner(0, lambda copy: copy.start())
    each_corner(0, lambda copy: copy.wait_recv())

    def row_step(part, carry):
        spots = [(g % 2, part * part_lon + g // 2) for g in range(2 * part_lon)]
        transform([(side * (tile_lat - 1), j) for side, j in spots], lambda n: spots[n])
        for index in range(2):
            where_exists(WAYS[index], lambda index=index: row_copy(index, part).start())
        return carry

    lax.fori_loop(0, row_parts, row_step, 0)
    for index in range(2):
        for part in range(1, 3):
            w_copy(index, part).start()

    def analyse(i, j):
        values = state_ref[i, j].astype(F32)
        mean = jnp.sum(values, axis=1, keepdims=True) * (1.0 / members)
        pert = (values - mean).astype(BF16)
        corner = quadrant_ref[i, pl.ds(j, 1), :]
        along = []
        for half, frac in (
            (corner // 2, frac_lat_ref[i, pl.ds(j, 1), :]),
            (corner % 2, frac_lon_ref[i, pl.ds(j, 1), :]),
        ):
            for a in range(3):
                along.append(
                    jnp.where(half == a, 1.0 - frac, 0.0) + jnp.where(half + 1 == a, frac, 0.0)
                )
        along.append(land_ref[i, pl.ds(j, 1), :].astype(F32))
        along.append(jnp.zeros_like(along[0]))
        coef = jnp.transpose(jnp.concatenate(along, axis=0))
        acc = mean
        for a in range(3):
            wide = jnp.concatenate([wbuf[i + a, j + b] for b in range(3)], axis=1)
            prod = nn(pert, wide)
            row = sum(
                coef[:, 3 + b : 4 + b] * prod[:, b * members : (b + 1) * members] for b in range(3)
            )
            acc = acc + coef[:, a : a + 1] * row
        result = jnp.where(coef[:, 6:7] == 1.0, acc, values)
        out_ref[i, j] = result.astype(BF16)

    def inner_step(t, carry):
        for g in range(group):
            analyse(*inner_place(t * group + g))
        return carry

    lax.fori_loop(0, g_inner, inner_step, 0)
    for index in range(2):
        for part in range(row_parts):
            received(index, lambda index, part=part: row_copy(index, part))
    each_corner(1, lambda copy: copy.start())
    for index in range(2):
        for part in range(3):
            w_copy(index, part).wait_recv()

    def side_step(t, carry):
        for g in range(group):
            analyse(*side_place(t * group + g))
        return carry

    lax.fori_loop(0, g_sides, side_step, 0)

    def unpack_step(t, carry):
        for g in range(2):
            for side in range(2):
                unpack(side, 1 + 2 * t + g)
        return carry

    lax.fori_loop(0, tile_lon // 2, unpack_step, 0)
    each_corner(1, lambda copy: copy.wait_recv())
    for side in range(2):
        for j in (0, tile_lon + 1):
            unpack(side, j)

    def rim_step(t, carry):
        for g in range(group):
            analyse(*row_place(t * group + g))
        return carry

    lax.fori_loop(0, g_rows, rim_step, 0)
    for index in range(len(WAYS)):
        sent(index, q_copy)
    for index in range(2):
        for part in range(3):
            w_copy(index, part).wait_send()
        for part in range(row_parts):
            sent(index, lambda index, part=part: row_copy(index, part))
    each_corner(0, lambda copy: copy.wait_send())
    each_corner(1, lambda copy: copy.wait_send())


VM = pl.BlockSpec(memory_space=pltpu.VMEM)


def body(counts, state, obs_row, obs_count, obs_value, obs_weight, quadrant, frac_lat, frac_lon, land):
    tile_lat, tile_lon, cells, members = state.shape
    rows = cells + SIDE_ROWS
    row_parts = 2 if tile_lon % 2 == 0 else 1
    qx = pl.pallas_call(
        prep_kernel,
        out_shape=jax.ShapeDtypeStruct((tile_lat, tile_lon, rows, members), BF16),
        in_specs=[pl.BlockSpec(memory_space=pltpu.SMEM)] + [VM] * 4,
        out_specs=VM,
        name="prep",
    )(obs_count, state, obs_row, obs_value, obs_weight)
    return pl.pallas_call(
        functools.partial(main_kernel, counts),
        out_shape=jax.ShapeDtypeStruct(state.shape, BF16),
        in_specs=[VM] * 6,
        out_specs=VM,
        scratch_shapes=[
            pltpu.VMEM((tile_lat + 2, tile_lon + 2, rows, members), BF16),
            pltpu.VMEM((tile_lat + 2, tile_lon + 2, members, members), BF16),
            pltpu.VMEM((2, tile_lon, members // 2 + SIDE_ROWS, members), BF16),
            pltpu.VMEM((2, tile_lon + 2, members // 2 + SIDE_ROWS, members), BF16),
            pltpu.SemaphoreType.DMA((4,)),
            pltpu.SemaphoreType.DMA((4,)),
            pltpu.SemaphoreType.DMA((2, 3)),
            pltpu.SemaphoreType.DMA((2, 3)),
            pltpu.SemaphoreType.DMA((2, row_parts)),
            pltpu.SemaphoreType.DMA((2, row_parts)),
            pltpu.SemaphoreType.DMA((2, 4)),
            pltpu.SemaphoreType.DMA((2, 4)),
        ],
        compiler_params=pltpu.CompilerParams(
            collective_id=0, has_side_effects=True, vmem_limit_bytes=48 * 1024 * 1024
        ),
        name="analyse",
    )(qx, state, quadrant, frac_lat, frac_lon, land)


def solution(mesh):
    counts = (mesh.shape["lat"], mesh.shape["lon"])
    return jax.shard_map(
        functools.partial(body, counts),
        mesh=mesh,
        in_specs=(
            P("lat", "lon", None, None),
            P("lat", "lon", None),
            P("lat", "lon"),
            P("lat", "lon", None),
            P("lat", "lon", None),
            P("lat", "lon", None),
            P("lat", "lon", None),
            P("lat", "lon", None),
            P("lat", "lon", None),
        ),
        out_specs=P("lat", "lon", None, None),
        check_vma=False,
    )
```

```python
import functools
import math

import jax
import jax.numpy as jnp
from jax import lax
from jax.experimental import pallas as pl
from jax.experimental.pallas import tpu as pltpu
from jax.sharding import PartitionSpec as P

ITERS = 6
NEAR = (0.5, 1.0, 0.5)
SIDE_ROWS = 8
F32 = jnp.float32
BF16 = jnp.bfloat16
MESH = pl.DeviceIdType.MESH
WAYS = ((-1, 0), (1, 0), (0, -1), (0, 1))
CORNERS = ((-1, -1), (-1, 1), (1, -1), (1, 1))


def nn(a, b):
    return lax.dot_general(a, b, (((1,), (0,)), ((), ())), preferred_element_type=F32)


def nt(a, b):
    return lax.dot_general(a, b, (((1,), (1,)), ((), ())), preferred_element_type=F32)


def tn(a, b):
    return lax.dot_general(a, b, (((0,), (0,)), ((), ())), preferred_element_type=F32)


def group_of(count, most=4):
    return next(g for g in range(most, 0, -1) if count % g == 0)


def main_kernel(
    counts, count_ref, state_in, row_in, value_in, weight_in, quadrant_in, frac_lat_in,
    frac_lon_in, land_in, result,
    state_ref, row_ref, value_ref, weight_ref, quadrant_ref, frac_lat_ref, frac_lon_ref,
    land_ref, out_ref, qbuf, wbuf, wpack, whalo, in_sem, out_sem, q_send, q_recv, w_send,
    w_recv, r_send, r_recv, c_send, c_recv,
):
    n_lat, n_lon = counts
    row_parts = r_send.shape[2]
    tile_lat, tile_lon, cells, members = state_ref.shape
    slots = row_ref.shape[-1]
    part_lon = tile_lon // row_parts
    lat, lon = lax.axis_index("lat"), lax.axis_index("lon")

    edge_rows = (pl.ds(0, 1), pl.ds(tile_lat - 1, 1), pl.ds(1, tile_lat - 2))
    loads = [
        pltpu.make_async_copy(state_in.at[rows], state_ref.at[rows], in_sem.at[n])
        for n, rows in enumerate(edge_rows)
    ]
    small = (
        (row_in, row_ref), (value_in, value_ref), (weight_in, weight_ref),
        (quadrant_in, quadrant_ref), (frac_lat_in, frac_lat_ref),
        (frac_lon_in, frac_lon_ref), (land_in, land_ref),
    )
    loads += [
        pltpu.make_async_copy(source, target, in_sem.at[3 + n])
        for n, (source, target) in enumerate(small)
    ]
    for n in (3, 4, 5, 0, 1, 2, 6, 7, 8, 9):
        loads[n].start()

    def exists(way):
        if way[0] < 0:
            return lat > 0
        if way[0] > 0:
            return lat < n_lat - 1
        return None

    def where_exists(way, do):
        if way[0] == 0:
            do()
        else:
            pl.when(exists(way))(do)

    def peer(way):
        return (lat + way[0], lax.rem(lon + way[1] + n_lon, n_lon))

    def remote(source, target, way, send, recv):
        return pltpu.make_async_remote_copy(
            src_ref=source,
            dst_ref=target,
            send_sem=send,
            recv_sem=recv,
            device_id=peer(way),
            device_id_type=MESH,
        )

    def column_of(part, t):
        if row_parts == 1:
            return t
        quarter = part_lon // 2
        return jnp.where(part == 0, quarter + t, t if t < quarter else t + part_lon)

    def q_lon(index):
        source, target = ((1, tile_lon + 1), (tile_lon, 0))[index]
        rows = pl.ds(1, tile_lat)
        return remote(
            qbuf.at[rows, source], qbuf.at[rows, target], WAYS[2 + index],
            q_send.at[index], q_recv.at[index],
        )

    def q_row(index, part):
        source, target = ((1, tile_lat + 1), (tile_lat, 0))[index]
        columns = pl.ds(1 + part * part_lon, part_lon)
        return remote(
            qbuf.at[source, columns], qbuf.at[target, columns], WAYS[index],
            r_send.at[0, index, part], r_recv.at[0, index, part],
        )

    def w_copy(index, part):
        way = WAYS[2 + index]
        source, target = (1, tile_lon + 1) if way[1] < 0 else (tile_lon, 0)
        rows = (pl.ds(2, tile_lat - 2), pl.ds(1, 1), pl.ds(tile_lat, 1))[part]
        return remote(
            wbuf.at[rows, source], wbuf.at[rows, target], way,
            w_send.at[index, part], w_recv.at[index, part],
        )

    def row_copy(index, part):
        columns = pl.ds(part * part_lon, part_lon)
        return remote(
            wpack.at[index, columns], whalo.at[1 - index, columns],
            WAYS[index], r_send.at[1, index, part], r_recv.at[1, index, part],
        )

    def corner_copy(stage, index):
        side, step = CORNERS[index]
        if stage == 0:
            row = 0 if side < 0 else tile_lat + 1
            source, target = (1, tile_lon + 1) if step < 0 else (tile_lon, 0)
            source, target = qbuf.at[row, source], qbuf.at[row, target]
        else:
            row = 0 if side < 0 else 1
            first = part_lon if row_parts == 2 else 0
            source, target = (first, tile_lon + 1) if step < 0 else (tile_lon - 1, tile_lon)
            source, target = whalo.at[row, source], whalo.at[row, target]
        return remote(
            source, target, (0, step), c_send.at[stage, index], c_recv.at[stage, index]
        )

    def each_corner(stage, do):
        for index, way in enumerate(CORNERS):
            where_exists(way, lambda index=index: do(corner_copy(stage, index)))

    barrier = pltpu.get_barrier_semaphore()
    for way in WAYS:
        where_exists(way, lambda way=way: pl.semaphore_signal(
            barrier, inc=1, device_id=peer(way), device_id_type=MESH))
    present = 2 + (lat > 0).astype(jnp.int32) + (lat < n_lat - 1).astype(jnp.int32)
    @pl.when(lat == 0)
    def _():
        qbuf[0] = jnp.zeros(qbuf.shape[1:], BF16)
        whalo[0] = jnp.zeros(whalo.shape[1:], BF16)

    @pl.when(lat == n_lat - 1)
    def _():
        qbuf[tile_lat + 1] = jnp.zeros(qbuf.shape[1:], BF16)
        whalo[1] = jnp.zeros(whalo.shape[1:], BF16)

    def received(index, make):
        way = WAYS[index]
        back = (-way[0], -way[1])
        where_exists(back, lambda: make(index).wait_recv())

    def sent(index, make):
        where_exists(WAYS[index], lambda: make(index).wait_send())

    which = lax.broadcasted_iota(jnp.int32, (SIDE_ROWS, members), 0)
    flat = jnp.full((members, members), 1.0 / members, BF16)

    def prepare(i, j):
        values = state_ref[i, j]
        mean = nn(values, flat)
        pert = values.astype(F32) - mean
        spot = lax.broadcasted_iota(jnp.int32, (1, slots), 1)
        weight = jnp.where(spot < count_ref[i, j], weight_ref[i, pl.ds(j, 1), :], 0.0)
        square = weight * weight
        hit = row_ref[i, pl.ds(j, 1), :] == lax.broadcasted_iota(jnp.int32, (cells, slots), 0)
        hit = jnp.where(hit, 1.0, 0.0).astype(BF16)
        wide = []
        for row in (square, square * value_ref[i, pl.ds(j, 1), :]):
            high = row.astype(BF16).astype(F32)
            both = jnp.concatenate([high, row - high], axis=1)
            wide.append(jnp.broadcast_to(both, (members, 2 * slots)).astype(BF16))
        sums = nt(jnp.concatenate([hit, hit], axis=1), jnp.concatenate(wide, axis=0))
        density, pulled = sums[:, :members], sums[:, members:]
        qbuf[i + 1, j + 1, pl.ds(0, cells), :] = (jnp.sqrt(density) * pert).astype(BF16)
        side = jnp.sum(pert * (pulled - density * mean), axis=0, keepdims=True)
        high = side.astype(BF16).astype(F32)
        tail = jnp.where(which == 0, high, jnp.where(which == 1, side - high, 0.0))
        qbuf[i + 1, j + 1, pl.ds(cells, SIDE_ROWS), :] = tail.astype(BF16)

    eye = (
        lax.broadcasted_iota(jnp.int32, (members, members), 0)
        == lax.broadcasted_iota(jnp.int32, (members, members), 1)
    ).astype(F32)

    line = lax.broadcasted_iota(jnp.int32, (members // 2, members), 0)
    lane = lax.broadcasted_iota(jnp.int32, (members // 2, members), 1)
    upper = lane >= line

    def through(row, matrix):
        high = row.astype(BF16).astype(F32)
        rows = jnp.where(which == 0, high, jnp.where(which == 1, row - high, 0.0))
        return jnp.sum(nn(rows.astype(BF16), matrix), axis=0, keepdims=True)

    def column(row):
        return jnp.transpose(jnp.broadcast_to(row, (members, members)))

    def gram_of(i, j):
        left, right = [], []
        tail = jnp.zeros((SIDE_ROWS, members), F32)
        for b in range(3):
            for a in range(3):
                scale = NEAR[a] * NEAR[b]
                block = qbuf[i + a, j + b, pl.ds(0, cells), :]
                right.append(block)
                left.append(block if scale == 1.0 else block * jnp.asarray(scale, BF16))
                tail += scale * qbuf[i + a, j + b, pl.ds(cells, SIDE_ROWS), :].astype(F32)
        gram = tn(jnp.concatenate(left, axis=0), jnp.concatenate(right, axis=0))
        return gram, jnp.sum(tail, axis=0, keepdims=True)

    def total(x):
        return jnp.sum(jnp.sum(x, axis=0, keepdims=True), axis=1, keepdims=True)

    def pair_factor(scale):
        first = 1.5 - 0.5 * scale
        r = 0.5 * scale / first
        middle = scale * first * first
        second = 1.5 - 0.5 * middle
        q = 0.5 * middle / second
        p1, p2, p3 = 1.0 - 2.0 * r, r * r - 2.0 * r, r * r
        coefs = (-r - q * p1, q * (r * p1 - p2), q * (r * p2 - p3), q * r * p3)
        both = first * second
        return both, coefs, scale * both * both

    def transform(places, pack_at=None):
        pack = pack_at is not None
        group = range(len(places))
        xs, sides, scalars = [], [], []
        for i, j in places:
            gram, side = gram_of(i, j)
            ridge = members - 1.0
            trace = total(gram * eye)
            frob = jnp.sqrt(total(gram * gram) + 2.0 * ridge * trace + ridge * ridge * members)
            centre = ridge + trace * (1.0 / members)
            inv = 1.0 / centre
            xs.append(gram * inv + eye * (ridge * inv - 1.0))
            sides.append(side)
            scale = centre / frob
            root, steps = 1.0, []
            for _ in range(ITERS // 2):
                both, coefs, scale = pair_factor(scale)
                root = root * both
                steps.append(coefs)
            scalars.append((frob, root, steps))
        zs = [None for _ in group]
        for step in range(ITERS // 2):
            last = step == ITERS // 2 - 1
            squares, ds, gs = [], [], []
            for x in xs:
                xb = x.astype(BF16)
                squares.append(nn(xb, xb))
            for n in group:
                a1, a2, a3, a4 = scalars[n][2][step]
                x, s = xs[n], squares[n]
                tail = nn(s.astype(BF16), (a3 * x + a4 * s).astype(BF16))
                ds.append(a1 * x + a2 * s + tail)
            for n in group:
                d = ds[n]
                db = d.astype(BF16)
                if not last:
                    gs.append((xs[n] + d) + nn(db, xs[n].astype(BF16)))
                zs[n] = d if step == 0 else (zs[n] + d) + nn(db, zs[n].astype(BF16))
            if not last:
                xs = [(gs[n] + ds[n]) + nn(ds[n].astype(BF16), gs[n].astype(BF16)) for n in group]
        for n, (i, j) in enumerate(places):
            frob, root, _ = scalars[n]
            zb = zs[n].astype(BF16)
            inner = sides[n] + through(sides[n], zb)
            inner = inner * (root * root / frob)
            mean_weight = inner + through(inner, zb)
            spread = math.sqrt(members - 1) * root / jnp.sqrt(frob)
            part = spread * (zs[n] + eye)
            wbuf[i + 1, j + 1] = (part + column(mean_weight)).astype(BF16)
            if pack:
                half = members // 2
                swapped = jnp.concatenate([part[half:, half:], part[half:, :half]], axis=1)
                wpack[pack_at(n)[0], pack_at(n)[1], pl.ds(0, half), :] = jnp.where(
                    upper, part[:half], swapped
                ).astype(BF16)
                diagonal = jnp.sum(part * eye, axis=0, keepdims=True)
                high = mean_weight.astype(BF16).astype(F32)
                wpack[pack_at(n)[0], pack_at(n)[1], pl.ds(half, SIDE_ROWS), :] = jnp.where(
                    which == 0, diagonal,
                    jnp.where(which == 1, high, jnp.where(which == 2, mean_weight - high, 0.0)),
                ).astype(BF16)

    def unpack(side, spot, j):
        half = members // 2
        sent = whalo[side, spot, pl.ds(0, half), :]
        tail = whalo[side, spot, pl.ds(half, SIDE_ROWS), :].astype(F32)
        turned = jnp.transpose(jnp.concatenate([sent, sent], axis=0)).astype(F32)
        sent = sent.astype(F32)
        swapped = jnp.concatenate([sent[:, half:], sent[:, :half]], axis=1)
        top = jnp.where(upper, sent, turned[:half])
        low = jnp.where(lane >= half, jnp.where(lane - half < line, swapped, turned[:half]), turned[half:])
        low = jnp.where(lane - half == line, tail[0:1], low)
        whole = jnp.concatenate([top, low], axis=0) + column(tail[1:2] + tail[2:3])
        wbuf[side * (tile_lat + 1), j] = whole.astype(BF16)

    mid_lat, mid_lon = tile_lat - 2, tile_lon - 2
    n_rows, n_sides, n_inner = 2 * tile_lon, 2 * mid_lat, mid_lat * mid_lon
    group = next(g for g in (4, 2) if all(n % g == 0 for n in (n_rows, n_sides, n_inner)))
    g_rows, g_sides, g_inner = n_rows // group, n_sides // group, n_inner // group
    wide = next(g for g in range(16, 0, -1) if mid_lat * tile_lon % g == 0)
    w_rest = mid_lat * tile_lon // wide
    ready = next(g for g in range(8, 0, -1) if mid_lat * tile_lon % g == 0)

    def row_place(k):
        return (k % 2) * (tile_lat - 1), k // 2

    def side_place(k):
        return 1 + k // 2, (k % 2) * (tile_lon - 1)

    def inner_place(k):
        return 1 + k // mid_lon, 1 + k % mid_lon

    for n in (3, 4, 5, 0, 1):
        loads[n].wait()

    def first_step(t, carry):
        for g in range(2 * part_lon):
            prepare((g % 2) * (tile_lat - 1), t * part_lon + g // 2)

        @pl.when(t == 0)
        def _():
            pl.semaphore_wait(barrier, present)

        for index in range(2):
            where_exists(WAYS[index], lambda index=index: q_row(index, t).start())
        return carry

    lax.fori_loop(0, row_parts, first_step, 0)
    loads[2].wait()

    def ready_step(t, carry):
        for g in range(ready):
            k = t * ready + g
            prepare(1 + k // tile_lon, k % tile_lon)
        return carry

    lax.fori_loop(0, mid_lat * tile_lon // ready, ready_step, 0)
    for index in range(2):
        q_lon(index).start()
    for index in range(2):
        q_lon(index).wait_recv()

    def rest_step(slot, carry):
        ks = [slot * wide + g for g in range(wide)]
        transform([(1 + k // tile_lon, k % tile_lon) for k in ks])
        return carry

    lax.fori_loop(0, w_rest, rest_step, 0)
    for index in range(2):
        w_copy(index, 0).start()
    for index in range(2):
        for part in range(row_parts):
            received(index, lambda index, part=part: q_row(index, part))
    each_corner(0, lambda copy: copy.start())

    def row_step(part, carry):
        @pl.when(part == row_parts - 1)
        def _():
            each_corner(0, lambda copy: copy.wait_recv())

        spots = [(g % 2, g // 2) for g in range(2 * part_lon)]
        transform(
            [(side * (tile_lat - 1), column_of(part, t)) for side, t in spots],
            lambda n: (spots[n][0], part * part_lon + spots[n][1]),
        )
        for index in range(2):
            where_exists(WAYS[index], lambda index=index: row_copy(index, part).start())
        return carry

    lax.fori_loop(0, row_parts, row_step, 0)
    for index in range(2):
        for part in range(1, 3):
            w_copy(index, part).start()

    def analyse(i, j):
        values = state_ref[i, j]
        mean = nn(values, flat)
        values = values.astype(F32)
        pert = (values - mean).astype(BF16)
        corner = quadrant_ref[i, pl.ds(j, 1), :]
        along = []
        for half, frac in (
            (corner // 2, frac_lat_ref[i, pl.ds(j, 1), :]),
            (corner % 2, frac_lon_ref[i, pl.ds(j, 1), :]),
        ):
            for a in range(3):
                along.append(
                    jnp.where(half == a, 1.0 - frac, 0.0) + jnp.where(half + 1 == a, frac, 0.0)
                )
        along.append(land_ref[i, pl.ds(j, 1), :].astype(F32))
        along.append(jnp.zeros_like(along[0]))
        coef = jnp.transpose(jnp.concatenate(along, axis=0))
        acc = mean
        for a in range(3):
            wide = jnp.concatenate([wbuf[i + a, j + b] for b in range(3)], axis=1)
            prod = nn(pert, wide)
            row = sum(
                coef[:, 3 + b : 4 + b] * prod[:, b * members : (b + 1) * members] for b in range(3)
            )
            acc = acc + coef[:, a : a + 1] * row
        result = jnp.where(coef[:, 6:7] == 1.0, acc, values)
        out_ref[i, j] = result.astype(BF16)

    for n in range(6, 10):
        loads[n].wait()
    middle = pl.ds(1, mid_lat)
    stores = [
        pltpu.make_async_copy(out_ref.at[rows, columns], result.at[rows, columns], out_sem.at[n])
        for n, (rows, columns) in enumerate((
            (middle, pl.ds(1, mid_lon)), (middle, pl.ds(0, 1)), (middle, pl.ds(tile_lon - 1, 1)),
            (pl.ds(0, 1), pl.ds(1, mid_lon)), (pl.ds(tile_lat - 1, 1), pl.ds(1, mid_lon)),
            (pl.ds(0, 1), pl.ds(0, 1)), (pl.ds(0, 1), pl.ds(tile_lon - 1, 1)),
            (pl.ds(tile_lat - 1, 1), pl.ds(0, 1)),
            (pl.ds(tile_lat - 1, 1), pl.ds(tile_lon - 1, 1)),
        ))
    ]

    def analyse_all(count, place):
        each = next(g for g in range(4, 0, -1) if count % g == 0)

        def step(t, carry):
            for g in range(each):
                analyse(*place(t * each + g))
            return carry

        lax.fori_loop(0, count // each, step, 0)

    analyse_all(n_inner, inner_place)
    stores[0].start()
    for index in range(2):
        for part in range(row_parts):
            received(index, lambda index, part=part: row_copy(index, part))
    each_corner(1, lambda copy: copy.start())
    for index in range(2):
        for part in range(3):
            w_copy(index, part).wait_recv()
    analyse_all(n_sides, side_place)
    stores[1].start()
    stores[2].start()

    def unpack_step(part, carry):
        for t in range(part_lon):
            for side in range(2):
                unpack(side, part * part_lon + t, 1 + column_of(part, t))
        return carry

    lax.fori_loop(0, row_parts, unpack_step, 0)
    analyse_all(n_rows - 4, lambda k: row_place(k + 2))
    stores[3].start()
    stores[4].start()
    each_corner(1, lambda copy: copy.wait_recv())
    for side in range(2):
        for n in range(2):
            unpack(side, tile_lon + n, n * (tile_lon + 1))
    analyse_all(4, lambda k: ((k % 2) * (tile_lat - 1), (k // 2) * (tile_lon - 1)))
    for n in range(5, 9):
        stores[n].start()
    for store in stores:
        store.wait()
    for index in range(2):
        q_lon(index).wait_send()
        for part in range(3):
            w_copy(index, part).wait_send()
        for part in range(row_parts):
            sent(index, lambda index, part=part: q_row(index, part))
            sent(index, lambda index, part=part: row_copy(index, part))
    each_corner(0, lambda copy: copy.wait_send())
    each_corner(1, lambda copy: copy.wait_send())


ANY = pl.BlockSpec(memory_space=pltpu.HBM)


def body(counts, state, obs_row, obs_count, obs_value, obs_weight, quadrant, frac_lat, frac_lon, land):
    tile_lat, tile_lon, cells, members = state.shape
    rows = cells + SIDE_ROWS
    row_parts = 2 if tile_lon % 4 == 0 else 1
    packed = members // 2 + SIDE_ROWS
    arrays = (state, obs_row, obs_value, obs_weight, quadrant, frac_lat, frac_lon, land)
    dma = pltpu.SemaphoreType.DMA
    return pl.pallas_call(
        functools.partial(main_kernel, counts),
        out_shape=jax.ShapeDtypeStruct(state.shape, BF16),
        in_specs=[pl.BlockSpec(memory_space=pltpu.SMEM)] + [ANY] * len(arrays),
        out_specs=ANY,
        scratch_shapes=[pltpu.VMEM(x.shape, x.dtype) for x in arrays] + [
            pltpu.VMEM(state.shape, BF16),
            pltpu.VMEM((tile_lat + 2, tile_lon + 2, rows, members), BF16),
            pltpu.VMEM((tile_lat + 2, tile_lon + 2, members, members), BF16),
            pltpu.VMEM((2, tile_lon, packed, members), BF16),
            pltpu.VMEM((2, tile_lon + 2, packed, members), BF16),
            dma((10,)),
            dma((9,)),
            dma((2,)),
            dma((2,)),
            dma((2, 3)),
            dma((2, 3)),
            dma((2, 2, row_parts)),
            dma((2, 2, row_parts)),
            dma((2, 4)),
            dma((2, 4)),
        ],
        compiler_params=pltpu.CompilerParams(
            collective_id=0, has_side_effects=True, vmem_limit_bytes=63 * 1024 * 1024
        ),
        name="analyse",
    )(obs_count, *arrays)


def solution(mesh):
    counts = (mesh.shape["lat"], mesh.shape["lon"])
    return jax.shard_map(
        functools.partial(body, counts),
        mesh=mesh,
        in_specs=(
            P("lat", "lon", None, None),
            P("lat", "lon", None),
            P("lat", "lon"),
            P("lat", "lon", None),
            P("lat", "lon", None),
            P("lat", "lon", None),
            P("lat", "lon", None),
            P("lat", "lon", None),
            P("lat", "lon", None),
        ),
        out_specs=P("lat", "lon", None, None),
        check_vma=False,
    )
```

```python
import functools
import math

import jax
import jax.numpy as jnp
from jax import lax
from jax.experimental import pallas as pl
from jax.experimental.pallas import tpu as pltpu
from jax.sharding import PartitionSpec as P

ITERS = 6
NEAR = (0.5, 1.0, 0.5)
SIDE_ROWS = 8
F32 = jnp.float32
BF16 = jnp.bfloat16
MESH = pl.DeviceIdType.MESH
WAYS = ((-1, 0), (1, 0), (0, -1), (0, 1))
CORNERS = ((-1, -1), (-1, 1), (1, -1), (1, 1))


def nn(a, b):
    return lax.dot_general(a, b, (((1,), (0,)), ((), ())), preferred_element_type=F32)


def nt(a, b):
    return lax.dot_general(a, b, (((1,), (1,)), ((), ())), preferred_element_type=F32)


def tn(a, b):
    return lax.dot_general(a, b, (((0,), (0,)), ((), ())), preferred_element_type=F32)


def group_of(count, most=4):
    return next(g for g in range(most, 0, -1) if count % g == 0)


def main_kernel(
    counts, count_in, state_in, row_in, value_in, weight_in, quadrant_in, frac_lat_in,
    frac_lon_in, land_in, out_ref,
    count_ref, state_ref, row_ref, value_ref, weight_ref, quadrant_ref, frac_lat_ref, frac_lon_ref,
    land_ref, qbuf, wbuf, wpack, whalo, in_sem, q_send, q_recv, w_send,
    w_recv, r_send, r_recv, c_send, c_recv,
):
    n_lat, n_lon = counts
    row_parts = r_send.shape[2]
    tile_lat, tile_lon, cells, members = state_ref.shape
    slots = row_ref.shape[-1]
    part_lon = tile_lon // row_parts
    lat, lon = lax.axis_index("lat"), lax.axis_index("lon")

    edge_rows = (pl.ds(0, 1), pl.ds(tile_lat - 1, 1), pl.ds(1, tile_lat - 2))
    loads = [
        pltpu.make_async_copy(state_in.at[rows], state_ref.at[rows], in_sem.at[n])
        for n, rows in enumerate(edge_rows)
    ]
    small = (
        (row_in, row_ref), (value_in, value_ref), (weight_in, weight_ref),
        (quadrant_in, quadrant_ref), (frac_lat_in, frac_lat_ref),
        (frac_lon_in, frac_lon_ref), (land_in, land_ref),
        (count_in, count_ref),
    )
    loads += [
        pltpu.make_async_copy(source, target, in_sem.at[3 + n])
        for n, (source, target) in enumerate(small)
    ]
    for n in (10, 3, 4, 5, 0, 1, 2, 6, 7, 8, 9):
        loads[n].start()

    def exists(way):
        if way[0] < 0:
            return lat > 0
        if way[0] > 0:
            return lat < n_lat - 1
        return None

    def where_exists(way, do):
        if way[0] == 0:
            do()
        else:
            pl.when(exists(way))(do)

    def peer(way):
        return (lat + way[0], lax.rem(lon + way[1] + n_lon, n_lon))

    def remote(source, target, way, send, recv):
        return pltpu.make_async_remote_copy(
            src_ref=source,
            dst_ref=target,
            send_sem=send,
            recv_sem=recv,
            device_id=peer(way),
            device_id_type=MESH,
        )

    def column_of(part, t):
        if row_parts == 1:
            return t
        quarter = part_lon // 2
        return jnp.where(part == 0, quarter + t, t if t < quarter else t + part_lon)

    def q_lon(index):
        source, target = ((1, tile_lon + 1), (tile_lon, 0))[index]
        rows = pl.ds(1, tile_lat)
        return remote(
            qbuf.at[rows, source], qbuf.at[rows, target], WAYS[2 + index],
            q_send.at[index], q_recv.at[index],
        )

    def q_row(index, part):
        source, target = ((1, tile_lat + 1), (tile_lat, 0))[index]
        columns = pl.ds(1 + part * part_lon, part_lon)
        return remote(
            qbuf.at[source, columns], qbuf.at[target, columns], WAYS[index],
            r_send.at[0, index, part], r_recv.at[0, index, part],
        )

    def w_copy(index, part):
        way = WAYS[2 + index]
        source, target = (1, tile_lon + 1) if way[1] < 0 else (tile_lon, 0)
        rows = (pl.ds(2, tile_lat - 2), pl.ds(1, 1), pl.ds(tile_lat, 1))[part]
        return remote(
            wbuf.at[rows, source], wbuf.at[rows, target], way,
            w_send.at[index, part], w_recv.at[index, part],
        )

    def row_copy(index, part):
        columns = pl.ds(part * part_lon, part_lon)
        return remote(
            wpack.at[index, columns], whalo.at[1 - index, columns],
            WAYS[index], r_send.at[1, index, part], r_recv.at[1, index, part],
        )

    def corner_copy(stage, index):
        side, step = CORNERS[index]
        if stage == 0:
            row = 0 if side < 0 else tile_lat + 1
            source, target = (1, tile_lon + 1) if step < 0 else (tile_lon, 0)
            source, target = qbuf.at[row, source], qbuf.at[row, target]
        else:
            row = 0 if side < 0 else 1
            first = part_lon if row_parts == 2 else 0
            source, target = (first, tile_lon + 1) if step < 0 else (tile_lon - 1, tile_lon)
            source, target = whalo.at[row, source], whalo.at[row, target]
        return remote(
            source, target, (0, step), c_send.at[stage, index], c_recv.at[stage, index]
        )

    def each_corner(stage, do):
        for index, way in enumerate(CORNERS):
            where_exists(way, lambda index=index: do(corner_copy(stage, index)))

    barrier = pltpu.get_barrier_semaphore()
    for way in WAYS:
        where_exists(way, lambda way=way: pl.semaphore_signal(
            barrier, inc=1, device_id=peer(way), device_id_type=MESH))
    present = 2 + (lat > 0).astype(jnp.int32) + (lat < n_lat - 1).astype(jnp.int32)
    @pl.when(lat == 0)
    def _():
        qbuf[0] = jnp.zeros(qbuf.shape[1:], BF16)
        whalo[0] = jnp.zeros(whalo.shape[1:], BF16)

    @pl.when(lat == n_lat - 1)
    def _():
        qbuf[tile_lat + 1] = jnp.zeros(qbuf.shape[1:], BF16)
        whalo[1] = jnp.zeros(whalo.shape[1:], BF16)

    def received(index, make):
        way = WAYS[index]
        back = (-way[0], -way[1])
        where_exists(back, lambda: make(index).wait_recv())

    def sent(index, make):
        where_exists(WAYS[index], lambda: make(index).wait_send())

    which = lax.broadcasted_iota(jnp.int32, (SIDE_ROWS, members), 0)
    flat = jnp.full((members, members), 1.0 / members, BF16)

    def prepare(i, j):
        values = state_ref[i, j]
        mean = nn(values, flat)
        pert = values.astype(F32) - mean
        spot = lax.broadcasted_iota(jnp.int32, (1, slots), 1)
        weight = jnp.where(spot < count_ref[i, j], weight_ref[i, pl.ds(j, 1), :], 0.0)
        square = weight * weight
        hit = row_ref[i, pl.ds(j, 1), :] == lax.broadcasted_iota(jnp.int32, (cells, slots), 0)
        hit = jnp.where(hit, 1.0, 0.0).astype(BF16)
        wide = []
        for row in (square, square * value_ref[i, pl.ds(j, 1), :]):
            high = row.astype(BF16).astype(F32)
            both = jnp.concatenate([high, row - high], axis=1)
            wide.append(jnp.broadcast_to(both, (members, 2 * slots)).astype(BF16))
        sums = nt(jnp.concatenate([hit, hit], axis=1), jnp.concatenate(wide, axis=0))
        density, pulled = sums[:, :members], sums[:, members:]
        qbuf[i + 1, j + 1, pl.ds(0, cells), :] = (jnp.sqrt(density) * pert).astype(BF16)
        side = jnp.sum(pert * (pulled - density * mean), axis=0, keepdims=True)
        high = side.astype(BF16).astype(F32)
        tail = jnp.where(which == 0, high, jnp.where(which == 1, side - high, 0.0))
        qbuf[i + 1, j + 1, pl.ds(cells, SIDE_ROWS), :] = tail.astype(BF16)

    eye = (
        lax.broadcasted_iota(jnp.int32, (members, members), 0)
        == lax.broadcasted_iota(jnp.int32, (members, members), 1)
    ).astype(F32)

    line = lax.broadcasted_iota(jnp.int32, (members // 2, members), 0)
    lane = lax.broadcasted_iota(jnp.int32, (members // 2, members), 1)
    upper = lane >= line

    def through(row, matrix):
        high = row.astype(BF16).astype(F32)
        rows = jnp.where(which == 0, high, jnp.where(which == 1, row - high, 0.0))
        return jnp.sum(nn(rows.astype(BF16), matrix), axis=0, keepdims=True)

    def column(row):
        return jnp.transpose(jnp.broadcast_to(row, (members, members)))

    def gram_of(i, j):
        left, right = [], []
        tail = jnp.zeros((SIDE_ROWS, members), F32)
        for b in range(3):
            for a in range(3):
                scale = NEAR[a] * NEAR[b]
                block = qbuf[i + a, j + b, pl.ds(0, cells), :]
                right.append(block)
                left.append(block if scale == 1.0 else block * jnp.asarray(scale, BF16))
                tail += scale * qbuf[i + a, j + b, pl.ds(cells, SIDE_ROWS), :].astype(F32)
        gram = tn(jnp.concatenate(left, axis=0), jnp.concatenate(right, axis=0))
        return gram, jnp.sum(tail, axis=0, keepdims=True)

    def total(x):
        return jnp.sum(jnp.sum(x, axis=0, keepdims=True), axis=1, keepdims=True)

    def pair_factor(scale):
        first = 1.5 - 0.5 * scale
        r = 0.5 * scale / first
        middle = scale * first * first
        second = 1.5 - 0.5 * middle
        q = 0.5 * middle / second
        p1, p2, p3 = 1.0 - 2.0 * r, r * r - 2.0 * r, r * r
        coefs = (-r - q * p1, q * (r * p1 - p2), q * (r * p2 - p3), q * r * p3)
        both = first * second
        return both, coefs, scale * both * both

    def transform(places, pack_at=None):
        pack = pack_at is not None
        group = range(len(places))
        xs, sides, scalars = [], [], []
        for i, j in places:
            gram, side = gram_of(i, j)
            ridge = members - 1.0
            trace = total(gram * eye)
            frob = jnp.sqrt(total(gram * gram) + 2.0 * ridge * trace + ridge * ridge * members)
            centre = ridge + trace * (1.0 / members)
            inv = 1.0 / centre
            xs.append(gram * inv + eye * (ridge * inv - 1.0))
            sides.append(side)
            scale = centre / frob
            root, steps = 1.0, []
            for _ in range(ITERS // 2):
                both, coefs, scale = pair_factor(scale)
                root = root * both
                steps.append(coefs)
            scalars.append((frob, root, steps))
        zs = [None for _ in group]
        for step in range(ITERS // 2):
            last = step == ITERS // 2 - 1
            squares, ds, gs = [], [], []
            for x in xs:
                xb = x.astype(BF16)
                squares.append(nn(xb, xb))
            for n in group:
                a1, a2, a3, a4 = scalars[n][2][step]
                x, s = xs[n], squares[n]
                tail = nn(s.astype(BF16), (a3 * x + a4 * s).astype(BF16))
                ds.append(a1 * x + a2 * s + tail)
            for n in group:
                d = ds[n]
                db = d.astype(BF16)
                if not last:
                    gs.append((xs[n] + d) + nn(db, xs[n].astype(BF16)))
                zs[n] = d if step == 0 else (zs[n] + d) + nn(db, zs[n].astype(BF16))
            if not last:
                xs = [(gs[n] + ds[n]) + nn(ds[n].astype(BF16), gs[n].astype(BF16)) for n in group]
        for n, (i, j) in enumerate(places):
            frob, root, _ = scalars[n]
            zb = zs[n].astype(BF16)
            inner = sides[n] + through(sides[n], zb)
            inner = inner * (root * root / frob)
            mean_weight = inner + through(inner, zb)
            spread = math.sqrt(members - 1) * root / jnp.sqrt(frob)
            part = spread * (zs[n] + eye)
            wbuf[i + 1, j + 1] = (part + column(mean_weight)).astype(BF16)
            if pack:
                half = members // 2
                swapped = jnp.concatenate([part[half:, half:], part[half:, :half]], axis=1)
                wpack[pack_at(n)[0], pack_at(n)[1], pl.ds(0, half), :] = jnp.where(
                    upper, part[:half], swapped
                ).astype(BF16)
                diagonal = jnp.sum(part * eye, axis=0, keepdims=True)
                high = mean_weight.astype(BF16).astype(F32)
                wpack[pack_at(n)[0], pack_at(n)[1], pl.ds(half, SIDE_ROWS), :] = jnp.where(
                    which == 0, diagonal,
                    jnp.where(which == 1, high, jnp.where(which == 2, mean_weight - high, 0.0)),
                ).astype(BF16)

    def unpack(side, spot, j):
        half = members // 2
        sent = whalo[side, spot, pl.ds(0, half), :]
        tail = whalo[side, spot, pl.ds(half, SIDE_ROWS), :].astype(F32)
        turned = jnp.transpose(jnp.concatenate([sent, sent], axis=0)).astype(F32)
        sent = sent.astype(F32)
        swapped = jnp.concatenate([sent[:, half:], sent[:, :half]], axis=1)
        top = jnp.where(upper, sent, turned[:half])
        low = jnp.where(lane >= half, jnp.where(lane - half < line, swapped, turned[:half]), turned[half:])
        low = jnp.where(lane - half == line, tail[0:1], low)
        whole = jnp.concatenate([top, low], axis=0) + column(tail[1:2] + tail[2:3])
        wbuf[side * (tile_lat + 1), j] = whole.astype(BF16)

    mid_lat, mid_lon = tile_lat - 2, tile_lon - 2
    n_rows, n_sides, n_inner = 2 * tile_lon, 2 * mid_lat, mid_lat * mid_lon
    group = next(g for g in (4, 2) if all(n % g == 0 for n in (n_rows, n_sides, n_inner)))
    g_rows, g_sides, g_inner = n_rows // group, n_sides // group, n_inner // group
    wide = next(g for g in range(16, 0, -1) if mid_lat * tile_lon % g == 0)
    w_rest = mid_lat * tile_lon // wide
    ready = next(g for g in range(8, 0, -1) if mid_lat * tile_lon % g == 0)

    def row_place(k):
        return (k % 2) * (tile_lat - 1), k // 2

    def side_place(k):
        return 1 + k // 2, (k % 2) * (tile_lon - 1)

    def inner_place(k):
        return 1 + k // mid_lon, 1 + k % mid_lon

    for n in (10, 3, 4, 5, 0, 1):
        loads[n].wait()

    def first_step(t, carry):
        for g in range(2 * part_lon):
            prepare((g % 2) * (tile_lat - 1), t * part_lon + g // 2)

        @pl.when(t == 0)
        def _():
            pl.semaphore_wait(barrier, present)

        for index in range(2):
            where_exists(WAYS[index], lambda index=index: q_row(index, t).start())
        return carry

    lax.fori_loop(0, row_parts, first_step, 0)
    loads[2].wait()

    def ready_step(t, carry):
        for g in range(ready):
            k = t * ready + g
            prepare(1 + k // tile_lon, k % tile_lon)
        return carry

    lax.fori_loop(0, mid_lat * tile_lon // ready, ready_step, 0)
    for index in range(2):
        q_lon(index).start()
    for index in range(2):
        q_lon(index).wait_recv()

    def rest_step(slot, carry):
        ks = [slot * wide + g for g in range(wide)]
        transform([(1 + k // tile_lon, k % tile_lon) for k in ks])
        return carry

    lax.fori_loop(0, w_rest, rest_step, 0)
    for index in range(2):
        w_copy(index, 0).start()
    for index in range(2):
        for part in range(row_parts):
            received(index, lambda index, part=part: q_row(index, part))
    each_corner(0, lambda copy: copy.start())

    def row_step(part, carry):
        @pl.when(part == row_parts - 1)
        def _():
            each_corner(0, lambda copy: copy.wait_recv())

        spots = [(g % 2, g // 2) for g in range(2 * part_lon)]
        transform(
            [(side * (tile_lat - 1), column_of(part, t)) for side, t in spots],
            lambda n: (spots[n][0], part * part_lon + spots[n][1]),
        )
        for index in range(2):
            where_exists(WAYS[index], lambda index=index: row_copy(index, part).start())
        return carry

    lax.fori_loop(0, row_parts, row_step, 0)
    for index in range(2):
        for part in range(1, 3):
            w_copy(index, part).start()

    def analyse(i, j):
        values = state_ref[i, j]
        mean = nn(values, flat)
        values = values.astype(F32)
        pert = (values - mean).astype(BF16)
        corner = quadrant_ref[i, pl.ds(j, 1), :]
        kept = land_ref[i, pl.ds(j, 1), :] != 1
        along = []
        for half, frac in (
            (corner // 2, frac_lat_ref[i, pl.ds(j, 1), :]),
            (corner % 2, frac_lon_ref[i, pl.ds(j, 1), :]),
        ):
            along.append(jnp.where(half == 0, 1.0 - frac, 0.0))
            along.append(jnp.where(half == 1, frac, 0.0))
        along[0] = jnp.where(kept, 2.0, along[0])
        along += [jnp.zeros_like(along[1])] * 4
        coef = jnp.transpose(jnp.concatenate(along, axis=0))
        edges = [jnp.broadcast_to(coef[:, n : n + 1], (cells, members)) for n in range(4)]
        kept = edges[0] > 1.5
        spread_lat = (edges[0], 1.0 - edges[0] - edges[1], edges[1])
        spread_lon = (edges[2], 1.0 - edges[2] - edges[3], edges[3])
        acc = mean
        for a in range(3):
            wide = jnp.concatenate([wbuf[i + a, j + b] for b in range(3)], axis=1)
            prod = nn(pert, wide)
            row = sum(
                spread_lon[b] * prod[:, b * members : (b + 1) * members] for b in range(3)
            )
            acc = acc + spread_lat[a] * row
        out_ref[i, j] = jnp.where(kept, values, acc).astype(BF16)

    for n in range(6, 10):
        loads[n].wait()
    def analyse_all(count, place):
        each = next(g for g in range(12, 0, -1) if count % g == 0)

        def step(t, carry):
            for g in range(each):
                analyse(*place(t * each + g))
            return carry

        lax.fori_loop(0, count // each, step, 0)

    analyse_all(n_inner, inner_place)
    for index in range(2):
        for part in range(row_parts):
            received(index, lambda index, part=part: row_copy(index, part))
    each_corner(1, lambda copy: copy.start())
    for index in range(2):
        for part in range(3):
            w_copy(index, part).wait_recv()
    analyse_all(n_sides, side_place)

    def unpack_step(part, carry):
        for t in range(part_lon):
            for side in range(2):
                unpack(side, part * part_lon + t, 1 + column_of(part, t))
        return carry

    lax.fori_loop(0, row_parts, unpack_step, 0)
    analyse_all(n_rows - 4, lambda k: row_place(k + 2))
    each_corner(1, lambda copy: copy.wait_recv())
    for side in range(2):
        for n in range(2):
            unpack(side, tile_lon + n, n * (tile_lon + 1))
    analyse_all(4, lambda k: ((k % 2) * (tile_lat - 1), (k // 2) * (tile_lon - 1)))
    for index in range(2):
        q_lon(index).wait_send()
        for part in range(3):
            w_copy(index, part).wait_send()
        for part in range(row_parts):
            sent(index, lambda index, part=part: q_row(index, part))
            sent(index, lambda index, part=part: row_copy(index, part))
    each_corner(0, lambda copy: copy.wait_send())
    each_corner(1, lambda copy: copy.wait_send())


ANY = pl.BlockSpec(memory_space=pltpu.HBM)


def body(counts, state, obs_row, obs_count, obs_value, obs_weight, quadrant, frac_lat, frac_lon, land):
    tile_lat, tile_lon, cells, members = state.shape
    rows = cells + SIDE_ROWS
    row_parts = 2 if tile_lon % 4 == 0 else 1
    packed = members // 2 + SIDE_ROWS
    hbm = pltpu.HBM
    arrays = (state, obs_row, obs_value, obs_weight, quadrant, frac_lat, frac_lon, land)
    dma = pltpu.SemaphoreType.DMA
    return pl.pallas_call(
        functools.partial(main_kernel, counts),
        out_shape=jax.ShapeDtypeStruct(state.shape, BF16),
        in_specs=[ANY] * (1 + len(arrays)),
        out_specs=pl.BlockSpec(memory_space=pltpu.VMEM),
        scratch_shapes=[pltpu.SMEM(obs_count.shape, obs_count.dtype)]
        + [pltpu.VMEM(x.shape, x.dtype) for x in arrays]
        + [
            pltpu.VMEM((tile_lat + 2, tile_lon + 2, rows, members), BF16),
            pltpu.VMEM((tile_lat + 2, tile_lon + 2, members, members), BF16),
            pltpu.VMEM((2, tile_lon, packed, members), BF16),
            pltpu.VMEM((2, tile_lon + 2, packed, members), BF16),
            dma((11,)),
            dma((2,)),
            dma((2,)),
            dma((2, 3)),
            dma((2, 3)),
            dma((2, 2, row_parts)),
            dma((2, 2, row_parts)),
            dma((2, 4)),
            dma((2, 4)),
        ],
        compiler_params=pltpu.CompilerParams(
            collective_id=0, has_side_effects=True, vmem_limit_bytes=48 * 1024 * 1024
        ),
        name="analyse",
    )(*(pltpu.with_memory_space_constraint(x, hbm) for x in (obs_count, *arrays)))


def solution(mesh):
    counts = (mesh.shape["lat"], mesh.shape["lon"])
    return jax.shard_map(
        functools.partial(body, counts),
        mesh=mesh,
        in_specs=(
            P("lat", "lon", None, None),
            P("lat", "lon", None),
            P("lat", "lon"),
            P("lat", "lon", None),
            P("lat", "lon", None),
            P("lat", "lon", None),
            P("lat", "lon", None),
            P("lat", "lon", None),
            P("lat", "lon", None),
        ),
        out_specs=P("lat", "lon", None, None),
        check_vma=False,
    )
```

```python
import functools
import math

import jax
import jax.numpy as jnp
from jax import lax
from jax.experimental import pallas as pl
from jax.experimental.pallas import tpu as pltpu
from jax.sharding import PartitionSpec as P

ITERS = 6
NEAR = (0.5, 1.0, 0.5)
SIDE_ROWS = 8
F32 = jnp.float32
BF16 = jnp.bfloat16
MESH = pl.DeviceIdType.MESH
WAYS = ((-1, 0), (1, 0), (0, -1), (0, 1))
CORNERS = ((-1, -1), (-1, 1), (1, -1), (1, 1))


def nn(a, b):
    return lax.dot_general(a, b, (((1,), (0,)), ((), ())), preferred_element_type=F32)


def nt(a, b):
    return lax.dot_general(a, b, (((1,), (1,)), ((), ())), preferred_element_type=F32)


def tn(a, b):
    return lax.dot_general(a, b, (((0,), (0,)), ((), ())), preferred_element_type=F32)


def group_of(count, most=4):
    return next(g for g in range(most, 0, -1) if count % g == 0)


def main_kernel(
    counts, count_in, state_in, row_in, value_in, weight_in, quadrant_in, frac_lat_in,
    frac_lon_in, land_in, out_ref,
    count_ref, state_ref, row_ref, value_ref, weight_ref, quadrant_ref, frac_lat_ref, frac_lon_ref,
    land_ref, acc_ref, share_ref, pert_ref, qbuf, wbuf, wpack, whalo, in_sem, q_send, q_recv, w_send,
    w_recv, r_send, r_recv, c_send, c_recv,
):
    n_lat, n_lon = counts
    row_parts = r_send.shape[2]
    tile_lat, tile_lon, cells, members = state_ref.shape
    slots = row_ref.shape[-1]
    part_lon = tile_lon // row_parts
    lat, lon = lax.axis_index("lat"), lax.axis_index("lon")

    edge_rows = (pl.ds(0, 1), pl.ds(tile_lat - 1, 1), pl.ds(1, tile_lat - 2))
    loads = [
        pltpu.make_async_copy(state_in.at[rows], state_ref.at[rows], in_sem.at[n])
        for n, rows in enumerate(edge_rows)
    ]
    small = (
        (row_in, row_ref), (value_in, value_ref), (weight_in, weight_ref),
        (quadrant_in, quadrant_ref), (frac_lat_in, frac_lat_ref),
        (frac_lon_in, frac_lon_ref), (land_in, land_ref),
        (count_in, count_ref),
    )
    loads += [
        pltpu.make_async_copy(source, target, in_sem.at[3 + n])
        for n, (source, target) in enumerate(small)
    ]
    for n in (10, 3, 4, 5, 0, 1, 2, 6, 7, 8, 9):
        loads[n].start()

    def exists(way):
        if way[0] < 0:
            return lat > 0
        if way[0] > 0:
            return lat < n_lat - 1
        return None

    def where_exists(way, do):
        if way[0] == 0:
            do()
        else:
            pl.when(exists(way))(do)

    def peer(way):
        return (lat + way[0], lax.rem(lon + way[1] + n_lon, n_lon))

    def remote(source, target, way, send, recv):
        return pltpu.make_async_remote_copy(
            src_ref=source,
            dst_ref=target,
            send_sem=send,
            recv_sem=recv,
            device_id=peer(way),
            device_id_type=MESH,
        )

    def column_of(part, t):
        if row_parts == 1:
            return t
        quarter = part_lon // 2
        return jnp.where(part == 0, quarter + t, t if t < quarter else t + part_lon)

    def q_lon(index):
        source, target = ((1, tile_lon + 1), (tile_lon, 0))[index]
        rows = pl.ds(1, tile_lat)
        return remote(
            qbuf.at[rows, source], qbuf.at[rows, target], WAYS[2 + index],
            q_send.at[index], q_recv.at[index],
        )

    def q_row(index, part):
        source, target = ((1, tile_lat + 1), (tile_lat, 0))[index]
        columns = pl.ds(1 + part * part_lon, part_lon)
        return remote(
            qbuf.at[source, columns], qbuf.at[target, columns], WAYS[index],
            r_send.at[0, index, part], r_recv.at[0, index, part],
        )

    def w_copy(index, part):
        way = WAYS[2 + index]
        source, target = (1, tile_lon + 1) if way[1] < 0 else (tile_lon, 0)
        rows = (pl.ds(2, tile_lat - 2), pl.ds(1, 1), pl.ds(tile_lat, 1))[part]
        return remote(
            wbuf.at[rows, source], wbuf.at[rows, target], way,
            w_send.at[index, part], w_recv.at[index, part],
        )

    def row_copy(index, part):
        columns = pl.ds(part * part_lon, part_lon)
        return remote(
            wpack.at[index, columns], whalo.at[1 - index, columns],
            WAYS[index], r_send.at[1, index, part], r_recv.at[1, index, part],
        )

    def corner_copy(stage, index):
        side, step = CORNERS[index]
        if stage == 0:
            row = 0 if side < 0 else tile_lat + 1
            source, target = (1, tile_lon + 1) if step < 0 else (tile_lon, 0)
            source, target = qbuf.at[row, source], qbuf.at[row, target]
        else:
            row = 0 if side < 0 else 1
            first = part_lon if row_parts == 2 else 0
            source, target = (first, tile_lon + 1) if step < 0 else (tile_lon - 1, tile_lon)
            source, target = whalo.at[row, source], whalo.at[row, target]
        return remote(
            source, target, (0, step), c_send.at[stage, index], c_recv.at[stage, index]
        )

    def each_corner(stage, do):
        for index, way in enumerate(CORNERS):
            where_exists(way, lambda index=index: do(corner_copy(stage, index)))

    barrier = pltpu.get_barrier_semaphore()
    for way in WAYS:
        where_exists(way, lambda way=way: pl.semaphore_signal(
            barrier, inc=1, device_id=peer(way), device_id_type=MESH))
    present = 2 + (lat > 0).astype(jnp.int32) + (lat < n_lat - 1).astype(jnp.int32)
    @pl.when(lat == 0)
    def _():
        qbuf[0] = jnp.zeros(qbuf.shape[1:], BF16)
        whalo[0] = jnp.zeros(whalo.shape[1:], BF16)

    @pl.when(lat == n_lat - 1)
    def _():
        qbuf[tile_lat + 1] = jnp.zeros(qbuf.shape[1:], BF16)
        whalo[1] = jnp.zeros(whalo.shape[1:], BF16)

    def received(index, make):
        way = WAYS[index]
        back = (-way[0], -way[1])
        where_exists(back, lambda: make(index).wait_recv())

    def sent(index, make):
        where_exists(WAYS[index], lambda: make(index).wait_send())

    which = lax.broadcasted_iota(jnp.int32, (SIDE_ROWS, members), 0)
    flat = jnp.full((members, members), 1.0 / members, BF16)

    def prepare(i, j):
        values = state_ref[i, j]
        mean = nn(values, flat)
        pert = values.astype(F32) - mean
        spot = lax.broadcasted_iota(jnp.int32, (1, slots), 1)
        weight = jnp.where(spot < count_ref[i, j], weight_ref[i, pl.ds(j, 1), :], 0.0)
        square = weight * weight
        hit = row_ref[i, pl.ds(j, 1), :] == lax.broadcasted_iota(jnp.int32, (cells, slots), 0)
        hit = jnp.where(hit, 1.0, 0.0).astype(BF16)
        wide = []
        for row in (square, square * value_ref[i, pl.ds(j, 1), :]):
            high = row.astype(BF16).astype(F32)
            both = jnp.concatenate([high, row - high], axis=1)
            wide.append(jnp.broadcast_to(both, (members, 2 * slots)).astype(BF16))
        sums = nt(jnp.concatenate([hit, hit], axis=1), jnp.concatenate(wide, axis=0))
        density, pulled = sums[:, :members], sums[:, members:]
        qbuf[i + 1, j + 1, pl.ds(0, cells), :] = (jnp.sqrt(density) * pert).astype(BF16)
        side = jnp.sum(pert * (pulled - density * mean), axis=0, keepdims=True)
        high = side.astype(BF16).astype(F32)
        tail = jnp.where(which == 0, high, jnp.where(which == 1, side - high, 0.0))
        qbuf[i + 1, j + 1, pl.ds(cells, SIDE_ROWS), :] = tail.astype(BF16)

    eye = (
        lax.broadcasted_iota(jnp.int32, (members, members), 0)
        == lax.broadcasted_iota(jnp.int32, (members, members), 1)
    ).astype(F32)

    line = lax.broadcasted_iota(jnp.int32, (members // 2, members), 0)
    lane = lax.broadcasted_iota(jnp.int32, (members // 2, members), 1)
    upper = lane >= line

    def through(row, matrix):
        high = row.astype(BF16).astype(F32)
        rows = jnp.where(which == 0, high, jnp.where(which == 1, row - high, 0.0))
        return jnp.sum(nn(rows.astype(BF16), matrix), axis=0, keepdims=True)

    def column(row):
        return jnp.transpose(jnp.broadcast_to(row, (members, members)))

    def gram_of(i, j):
        left, right = [], []
        tail = jnp.zeros((SIDE_ROWS, members), F32)
        for b in range(3):
            for a in range(3):
                scale = NEAR[a] * NEAR[b]
                block = qbuf[i + a, j + b, pl.ds(0, cells), :]
                right.append(block)
                left.append(block if scale == 1.0 else block * jnp.asarray(scale, BF16))
                tail += scale * qbuf[i + a, j + b, pl.ds(cells, SIDE_ROWS), :].astype(F32)
        gram = tn(jnp.concatenate(left, axis=0), jnp.concatenate(right, axis=0))
        return gram, jnp.sum(tail, axis=0, keepdims=True)

    def total(x):
        return jnp.sum(jnp.sum(x, axis=0, keepdims=True), axis=1, keepdims=True)

    def pair_factor(scale):
        first = 1.5 - 0.5 * scale
        r = 0.5 * scale / first
        middle = scale * first * first
        second = 1.5 - 0.5 * middle
        q = 0.5 * middle / second
        p1, p2, p3 = 1.0 - 2.0 * r, r * r - 2.0 * r, r * r
        coefs = (-r - q * p1, q * (r * p1 - p2), q * (r * p2 - p3), q * r * p3)
        both = first * second
        return both, coefs, scale * both * both

    def transform(places, pack_at=None):
        pack = pack_at is not None
        group = range(len(places))
        xs, sides, scalars = [], [], []
        for i, j in places:
            gram, side = gram_of(i, j)
            ridge = members - 1.0
            trace = total(gram * eye)
            frob = jnp.sqrt(total(gram * gram) + 2.0 * ridge * trace + ridge * ridge * members)
            centre = ridge + trace * (1.0 / members)
            inv = 1.0 / centre
            xs.append(gram * inv + eye * (ridge * inv - 1.0))
            sides.append(side)
            scale = centre / frob
            root, steps = 1.0, []
            for _ in range(ITERS // 2):
                both, coefs, scale = pair_factor(scale)
                root = root * both
                steps.append(coefs)
            scalars.append((frob, root, steps))
        zs = [None for _ in group]
        for step in range(ITERS // 2):
            last = step == ITERS // 2 - 1
            squares, ds, gs = [], [], []
            for x in xs:
                xb = x.astype(BF16)
                squares.append(nn(xb, xb))
            for n in group:
                a1, a2, a3, a4 = scalars[n][2][step]
                x, s = xs[n], squares[n]
                tail = nn(s.astype(BF16), (a3 * x + a4 * s).astype(BF16))
                ds.append(a1 * x + a2 * s + tail)
            for n in group:
                d = ds[n]
                db = d.astype(BF16)
                if not last:
                    gs.append((xs[n] + d) + nn(db, xs[n].astype(BF16)))
                zs[n] = d if step == 0 else (zs[n] + d) + nn(db, zs[n].astype(BF16))
            if not last:
                xs = [(gs[n] + ds[n]) + nn(ds[n].astype(BF16), gs[n].astype(BF16)) for n in group]
        for n, (i, j) in enumerate(places):
            frob, root, _ = scalars[n]
            zb = zs[n].astype(BF16)
            inner = sides[n] + through(sides[n], zb)
            inner = inner * (root * root / frob)
            mean_weight = inner + through(inner, zb)
            spread = math.sqrt(members - 1) * root / jnp.sqrt(frob)
            part = spread * (zs[n] + eye)
            wbuf[i + 1, j + 1] = (part + column(mean_weight)).astype(BF16)
            if pack:
                half = members // 2
                swapped = jnp.concatenate([part[half:, half:], part[half:, :half]], axis=1)
                wpack[pack_at(n)[0], pack_at(n)[1], pl.ds(0, half), :] = jnp.where(
                    upper, part[:half], swapped
                ).astype(BF16)
                diagonal = jnp.sum(part * eye, axis=0, keepdims=True)
                high = mean_weight.astype(BF16).astype(F32)
                wpack[pack_at(n)[0], pack_at(n)[1], pl.ds(half, SIDE_ROWS), :] = jnp.where(
                    which == 0, diagonal,
                    jnp.where(which == 1, high, jnp.where(which == 2, mean_weight - high, 0.0)),
                ).astype(BF16)

    def unpack(side, spot, j):
        half = members // 2
        sent = whalo[side, spot, pl.ds(0, half), :]
        tail = whalo[side, spot, pl.ds(half, SIDE_ROWS), :].astype(F32)
        turned = jnp.transpose(jnp.concatenate([sent, sent], axis=0)).astype(F32)
        sent = sent.astype(F32)
        swapped = jnp.concatenate([sent[:, half:], sent[:, :half]], axis=1)
        top = jnp.where(upper, sent, turned[:half])
        low = jnp.where(lane >= half, jnp.where(lane - half < line, swapped, turned[:half]), turned[half:])
        low = jnp.where(lane - half == line, tail[0:1], low)
        whole = jnp.concatenate([top, low], axis=0) + column(tail[1:2] + tail[2:3])
        wbuf[side * (tile_lat + 1), j] = whole.astype(BF16)

    mid_lat, mid_lon = tile_lat - 2, tile_lon - 2
    n_rows, n_sides, n_inner = 2 * tile_lon, 2 * mid_lat, mid_lat * mid_lon
    group = next(g for g in (4, 2) if all(n % g == 0 for n in (n_rows, n_sides, n_inner)))
    g_rows, g_sides, g_inner = n_rows // group, n_sides // group, n_inner // group
    wide = next(g for g in range(16, 0, -1) if mid_lat * tile_lon % g == 0)
    w_rest = mid_lat * tile_lon // wide
    ready = next(g for g in range(8, 0, -1) if mid_lat * tile_lon % g == 0)

    def row_place(k):
        return (k % 2) * (tile_lat - 1), k // 2

    def side_place(k):
        return 1 + k // 2, (k % 2) * (tile_lon - 1)

    def inner_place(k):
        return 1 + k // mid_lon, 1 + k % mid_lon

    for n in (10, 3, 4, 5, 0, 1):
        loads[n].wait()

    def first_step(t, carry):
        for g in range(2 * part_lon):
            prepare((g % 2) * (tile_lat - 1), t * part_lon + g // 2)

        @pl.when(t == 0)
        def _():
            pl.semaphore_wait(barrier, present)

        for index in range(2):
            where_exists(WAYS[index], lambda index=index: q_row(index, t).start())
        return carry

    lax.fori_loop(0, row_parts, first_step, 0)
    loads[2].wait()

    def ready_step(t, carry):
        for g in range(ready):
            k = t * ready + g
            prepare(1 + k // tile_lon, k % tile_lon)
        return carry

    lax.fori_loop(0, mid_lat * tile_lon // ready, ready_step, 0)
    for index in range(2):
        q_lon(index).start()
    for index in range(2):
        q_lon(index).wait_recv()

    def rest_step(slot, carry):
        ks = [slot * wide + g for g in range(wide)]
        transform([(1 + k // tile_lon, k % tile_lon) for k in ks])
        return carry

    lax.fori_loop(0, w_rest, rest_step, 0)
    for index in range(2):
        w_copy(index, 0).start()
    for index in range(2):
        for part in range(row_parts):
            received(index, lambda index, part=part: q_row(index, part))
    each_corner(0, lambda copy: copy.start())

    def row_step(part, carry):
        @pl.when(part == row_parts - 1)
        def _():
            each_corner(0, lambda copy: copy.wait_recv())

        spots = [(g % 2, g // 2) for g in range(2 * part_lon)]
        transform(
            [(side * (tile_lat - 1), column_of(part, t)) for side, t in spots],
            lambda n: (spots[n][0], part * part_lon + spots[n][1]),
        )
        for index in range(2):
            where_exists(WAYS[index], lambda index=index: row_copy(index, part).start())
        return carry

    lax.fori_loop(0, row_parts, row_step, 0)
    for index in range(2):
        for part in range(1, 3):
            w_copy(index, part).start()

    def analyse(i, j, side=None):
        values = state_ref[i, j]
        mean = nn(values, flat)
        values = values.astype(F32)
        pert = (values - mean).astype(BF16)
        corner = quadrant_ref[i, pl.ds(j, 1), :]
        kept = land_ref[i, pl.ds(j, 1), :] != 1
        along = []
        for half, frac in (
            (corner // 2, frac_lat_ref[i, pl.ds(j, 1), :]),
            (corner % 2, frac_lon_ref[i, pl.ds(j, 1), :]),
        ):
            along.append(jnp.where(half == 0, 1.0 - frac, 0.0))
            along.append(jnp.where(half == 1, frac, 0.0))
        along[0] = jnp.where(kept, 2.0, along[0])
        along += [jnp.zeros_like(along[1])] * 4
        coef = jnp.transpose(jnp.concatenate(along, axis=0))
        edges = [jnp.broadcast_to(coef[:, n : n + 1], (cells, members)) for n in range(4)]
        kept = edges[0] > 1.5
        spread_lat = (edges[0], 1.0 - edges[0] - edges[1], edges[1])
        spread_lon = (edges[2], 1.0 - edges[2] - edges[3], edges[3])
        halo = None if side is None else 2 * side
        acc = mean
        for a in range(3):
            if a == halo:
                continue
            wide = jnp.concatenate([wbuf[i + a, j + b] for b in range(3)], axis=1)
            prod = nn(pert, wide)
            row = sum(
                spread_lon[b] * prod[:, b * members : (b + 1) * members] for b in range(3)
            )
            acc = acc + spread_lat[a] * row
        acc = jnp.where(kept, values, acc)
        if side is None:
            out_ref[i, j] = acc.astype(BF16)
        else:
            share = jnp.where(kept, 0.0, spread_lat[halo])
            acc_ref[side, j] = acc
            pert_ref[side, j] = pert
            for b in range(3):
                share_ref[side, j, b] = share * spread_lon[b]

    def finish(side, j):
        i = side * (tile_lat - 1)
        wide = jnp.concatenate([wbuf[side * (tile_lat + 1), j + b] for b in range(3)], axis=1)
        prod = nn(pert_ref[side, j], wide)
        acc = acc_ref[side, j]
        for b in range(3):
            acc = acc + share_ref[side, j, b] * prod[:, b * members : (b + 1) * members]
        out_ref[i, j] = acc.astype(BF16)

    for n in range(6, 10):
        loads[n].wait()
    def analyse_all(count, place):
        each = next(g for g in range(12, 0, -1) if count % g == 0)

        def step(t, carry):
            for g in range(each):
                analyse(*place(t * each + g))
            return carry

        lax.fori_loop(0, count // each, step, 0)

    analyse_all(n_inner, inner_place)
    for index in range(2):
        for part in range(3):
            w_copy(index, part).wait_recv()
    each_own = next(g for g in (4, 2, 1) if tile_lon % g == 0)

    def own_step(t, carry):
        for g in range(each_own):
            for side in range(2):
                analyse(side * (tile_lat - 1), t * each_own + g, side)
        return carry

    lax.fori_loop(0, tile_lon // each_own, own_step, 0)
    for index in range(2):
        for part in range(row_parts):
            received(index, lambda index, part=part: row_copy(index, part))
    each_corner(1, lambda copy: copy.start())
    analyse_all(n_sides, side_place)

    def unpack_step(part, carry):
        for t in range(part_lon):
            for side in range(2):
                unpack(side, part * part_lon + t, 1 + column_of(part, t))
        return carry

    lax.fori_loop(0, row_parts, unpack_step, 0)
    for j in range(1, tile_lon - 1):
        for side in range(2):
            finish(side, j)
    each_corner(1, lambda copy: copy.wait_recv())
    for side in range(2):
        for n in range(2):
            unpack(side, tile_lon + n, n * (tile_lon + 1))
    for j in (0, tile_lon - 1):
        for side in range(2):
            finish(side, j)
    for index in range(2):
        q_lon(index).wait_send()
        for part in range(3):
            w_copy(index, part).wait_send()
        for part in range(row_parts):
            sent(index, lambda index, part=part: q_row(index, part))
            sent(index, lambda index, part=part: row_copy(index, part))
    each_corner(0, lambda copy: copy.wait_send())
    each_corner(1, lambda copy: copy.wait_send())


ANY = pl.BlockSpec(memory_space=pltpu.HBM)


def body(counts, state, obs_row, obs_count, obs_value, obs_weight, quadrant, frac_lat, frac_lon, land):
    tile_lat, tile_lon, cells, members = state.shape
    rows = cells + SIDE_ROWS
    row_parts = 2 if tile_lon % 4 == 0 else 1
    packed = members // 2 + SIDE_ROWS
    hbm = pltpu.HBM
    arrays = (state, obs_row, obs_value, obs_weight, quadrant, frac_lat, frac_lon, land)
    dma = pltpu.SemaphoreType.DMA
    return pl.pallas_call(
        functools.partial(main_kernel, counts),
        out_shape=jax.ShapeDtypeStruct(state.shape, BF16),
        in_specs=[ANY] * (1 + len(arrays)),
        out_specs=pl.BlockSpec(memory_space=pltpu.VMEM),
        scratch_shapes=[pltpu.SMEM(obs_count.shape, obs_count.dtype)]
        + [pltpu.VMEM(x.shape, x.dtype) for x in arrays]
        + [
            pltpu.VMEM((2, tile_lon, cells, members), F32),
            pltpu.VMEM((2, tile_lon, 3, cells, members), F32),
            pltpu.VMEM((2, tile_lon, cells, members), BF16),
            pltpu.VMEM((tile_lat + 2, tile_lon + 2, rows, members), BF16),
            pltpu.VMEM((tile_lat + 2, tile_lon + 2, members, members), BF16),
            pltpu.VMEM((2, tile_lon, packed, members), BF16),
            pltpu.VMEM((2, tile_lon + 2, packed, members), BF16),
            dma((11,)),
            dma((2,)),
            dma((2,)),
            dma((2, 3)),
            dma((2, 3)),
            dma((2, 2, row_parts)),
            dma((2, 2, row_parts)),
            dma((2, 4)),
            dma((2, 4)),
        ],
        compiler_params=pltpu.CompilerParams(
            collective_id=0, has_side_effects=True, vmem_limit_bytes=48 * 1024 * 1024
        ),
        name="analyse",
    )(*(pltpu.with_memory_space_constraint(x, hbm) for x in (obs_count, *arrays)))


def solution(mesh):
    counts = (mesh.shape["lat"], mesh.shape["lon"])
    return jax.shard_map(
        functools.partial(body, counts),
        mesh=mesh,
        in_specs=(
            P("lat", "lon", None, None),
            P("lat", "lon", None),
            P("lat", "lon"),
            P("lat", "lon", None),
            P("lat", "lon", None),
            P("lat", "lon", None),
            P("lat", "lon", None),
            P("lat", "lon", None),
            P("lat", "lon", None),
        ),
        out_specs=P("lat", "lon", None, None),
        check_vma=False,
    )
```

```python
import functools
import math

import jax
import jax.numpy as jnp
from jax import lax
from jax.experimental import pallas as pl
from jax.experimental.pallas import tpu as pltpu
from jax.sharding import PartitionSpec as P

ITERS = 6
NEAR = (0.5, 1.0, 0.5)
SIDE_ROWS = 8
F32 = jnp.float32
BF16 = jnp.bfloat16
MESH = pl.DeviceIdType.MESH
WAYS = ((-1, 0), (1, 0), (0, -1), (0, 1))
CORNERS = ((-1, -1), (-1, 1), (1, -1), (1, 1))


def nn(a, b):
    return lax.dot_general(a, b, (((1,), (0,)), ((), ())), preferred_element_type=F32)


def nt(a, b):
    return lax.dot_general(a, b, (((1,), (1,)), ((), ())), preferred_element_type=F32)


def tn(a, b):
    return lax.dot_general(a, b, (((0,), (0,)), ((), ())), preferred_element_type=F32)


def group_of(count, most=4):
    return next(g for g in range(most, 0, -1) if count % g == 0)


def main_kernel(
    counts, count_in, state_in, row_in, value_in, weight_in, quadrant_in, frac_lat_in,
    frac_lon_in, land_in, out_ref,
    count_ref, state_ref, row_ref, value_ref, weight_ref, quadrant_ref, frac_lat_ref, frac_lon_ref,
    land_ref, acc_ref, share_ref, pert_ref, qbuf, wbuf, wpack, whalo, in_sem, q_send, q_recv, w_send,
    w_recv, r_send, r_recv, c_send, c_recv,
):
    n_lat, n_lon = counts
    row_parts = r_send.shape[2]
    tile_lat, tile_lon, cells, members = state_ref.shape
    slots = row_ref.shape[-1]
    part_lon = tile_lon // row_parts
    lat, lon = lax.axis_index("lat"), lax.axis_index("lon")

    edge_rows = (pl.ds(0, 1), pl.ds(tile_lat - 1, 1), pl.ds(1, tile_lat - 2))
    loads = [
        pltpu.make_async_copy(state_in.at[rows], state_ref.at[rows], in_sem.at[n])
        for n, rows in enumerate(edge_rows)
    ]
    small = (
        (row_in, row_ref), (value_in, value_ref), (weight_in, weight_ref),
        (quadrant_in, quadrant_ref), (frac_lat_in, frac_lat_ref),
        (frac_lon_in, frac_lon_ref), (land_in, land_ref),
        (count_in, count_ref),
    )
    loads += [
        pltpu.make_async_copy(source, target, in_sem.at[3 + n])
        for n, (source, target) in enumerate(small)
    ]
    for n in (10, 3, 4, 5, 0, 1, 2, 6, 7, 8, 9):
        loads[n].start()

    def exists(way):
        if way[0] < 0:
            return lat > 0
        if way[0] > 0:
            return lat < n_lat - 1
        return None

    def where_exists(way, do):
        if way[0] == 0:
            do()
        else:
            pl.when(exists(way))(do)

    def peer(way):
        return (lat + way[0], lax.rem(lon + way[1] + n_lon, n_lon))

    def remote(source, target, way, send, recv):
        return pltpu.make_async_remote_copy(
            src_ref=source,
            dst_ref=target,
            send_sem=send,
            recv_sem=recv,
            device_id=peer(way),
            device_id_type=MESH,
        )

    def column_of(part, t):
        if row_parts == 1:
            return t
        quarter = part_lon // 2
        return jnp.where(part == 0, quarter + t, t if t < quarter else t + part_lon)

    def q_lon(index):
        source, target = ((1, tile_lon + 1), (tile_lon, 0))[index]
        rows = pl.ds(1, tile_lat)
        return remote(
            qbuf.at[rows, source], qbuf.at[rows, target], WAYS[2 + index],
            q_send.at[index], q_recv.at[index],
        )

    def q_row(index, part):
        source, target = ((1, tile_lat + 1), (tile_lat, 0))[index]
        columns = pl.ds(1 + part * part_lon, part_lon)
        return remote(
            qbuf.at[source, columns], qbuf.at[target, columns], WAYS[index],
            r_send.at[0, index, part], r_recv.at[0, index, part],
        )

    def w_copy(index, part):
        way = WAYS[2 + index]
        source, target = (1, tile_lon + 1) if way[1] < 0 else (tile_lon, 0)
        rows = (pl.ds(2, tile_lat - 2), pl.ds(1, 1), pl.ds(tile_lat, 1))[part]
        return remote(
            wbuf.at[rows, source], wbuf.at[rows, target], way,
            w_send.at[index, part], w_recv.at[index, part],
        )

    def row_copy(index, part):
        columns = pl.ds(part * part_lon, part_lon)
        return remote(
            wpack.at[index, columns], whalo.at[1 - index, columns],
            WAYS[index], r_send.at[1, index, part], r_recv.at[1, index, part],
        )

    def corner_copy(stage, index):
        side, step = CORNERS[index]
        if stage == 0:
            row = 0 if side < 0 else tile_lat + 1
            source, target = (1, tile_lon + 1) if step < 0 else (tile_lon, 0)
            source, target = qbuf.at[row, source], qbuf.at[row, target]
        else:
            row = 0 if side < 0 else 1
            first = part_lon if row_parts == 2 else 0
            source, target = (first, tile_lon + 1) if step < 0 else (tile_lon - 1, tile_lon)
            source, target = whalo.at[row, source], whalo.at[row, target]
        return remote(
            source, target, (0, step), c_send.at[stage, index], c_recv.at[stage, index]
        )

    def each_corner(stage, do):
        for index, way in enumerate(CORNERS):
            where_exists(way, lambda index=index: do(corner_copy(stage, index)))

    barrier = pltpu.get_barrier_semaphore()
    for way in WAYS:
        where_exists(way, lambda way=way: pl.semaphore_signal(
            barrier, inc=1, device_id=peer(way), device_id_type=MESH))
    present = 2 + (lat > 0).astype(jnp.int32) + (lat < n_lat - 1).astype(jnp.int32)
    @pl.when(lat == 0)
    def _():
        qbuf[0] = jnp.zeros(qbuf.shape[1:], BF16)
        whalo[0] = jnp.zeros(whalo.shape[1:], BF16)

    @pl.when(lat == n_lat - 1)
    def _():
        qbuf[tile_lat + 1] = jnp.zeros(qbuf.shape[1:], BF16)
        whalo[1] = jnp.zeros(whalo.shape[1:], BF16)

    def received(index, make):
        way = WAYS[index]
        back = (-way[0], -way[1])
        where_exists(back, lambda: make(index).wait_recv())

    def sent(index, make):
        where_exists(WAYS[index], lambda: make(index).wait_send())

    which = lax.broadcasted_iota(jnp.int32, (SIDE_ROWS, members), 0)
    flat = jnp.full((members, members), 1.0 / members, BF16)

    def prepare(i, j):
        values = state_ref[i, j]
        mean = nn(values, flat)
        pert = values.astype(F32) - mean
        spot = lax.broadcasted_iota(jnp.int32, (1, slots), 1)
        weight = jnp.where(spot < count_ref[i, j], weight_ref[i, pl.ds(j, 1), :], 0.0)
        square = weight * weight
        hit = row_ref[i, pl.ds(j, 1), :] == lax.broadcasted_iota(jnp.int32, (cells, slots), 0)
        hit = jnp.where(hit, 1.0, 0.0).astype(BF16)
        wide = []
        for row in (square, square * value_ref[i, pl.ds(j, 1), :]):
            high = row.astype(BF16).astype(F32)
            both = jnp.concatenate([high, row - high], axis=1)
            wide.append(jnp.broadcast_to(both, (members, 2 * slots)).astype(BF16))
        sums = nt(jnp.concatenate([hit, hit], axis=1), jnp.concatenate(wide, axis=0))
        density, pulled = sums[:, :members], sums[:, members:]
        qbuf[i + 1, j + 1, pl.ds(0, cells), :] = (jnp.sqrt(density) * pert).astype(BF16)
        side = jnp.sum(pert * (pulled - density * mean), axis=0, keepdims=True)
        high = side.astype(BF16).astype(F32)
        tail = jnp.where(which == 0, high, jnp.where(which == 1, side - high, 0.0))
        qbuf[i + 1, j + 1, pl.ds(cells, SIDE_ROWS), :] = tail.astype(BF16)

    eye = (
        lax.broadcasted_iota(jnp.int32, (members, members), 0)
        == lax.broadcasted_iota(jnp.int32, (members, members), 1)
    ).astype(F32)

    line = lax.broadcasted_iota(jnp.int32, (members // 2, members), 0)
    lane = lax.broadcasted_iota(jnp.int32, (members // 2, members), 1)
    upper = lane >= line

    def through(row, matrix):
        high = row.astype(BF16).astype(F32)
        rows = jnp.where(which == 0, high, jnp.where(which == 1, row - high, 0.0))
        return jnp.sum(nn(rows.astype(BF16), matrix), axis=0, keepdims=True)

    def column(row):
        return jnp.transpose(jnp.broadcast_to(row, (members, members)))

    def gram_of(i, j):
        left, right = [], []
        tail = jnp.zeros((SIDE_ROWS, members), F32)
        for b in range(3):
            for a in range(3):
                scale = NEAR[a] * NEAR[b]
                block = qbuf[i + a, j + b, pl.ds(0, cells), :]
                right.append(block)
                left.append(block if scale == 1.0 else block * jnp.asarray(scale, BF16))
                tail += scale * qbuf[i + a, j + b, pl.ds(cells, SIDE_ROWS), :].astype(F32)
        gram = tn(jnp.concatenate(left, axis=0), jnp.concatenate(right, axis=0))
        return gram, jnp.sum(tail, axis=0, keepdims=True)

    def total(x):
        return jnp.sum(jnp.sum(x, axis=0, keepdims=True), axis=1, keepdims=True)

    def pair_factor(scale):
        first = 1.5 - 0.5 * scale
        r = 0.5 * scale / first
        middle = scale * first * first
        second = 1.5 - 0.5 * middle
        q = 0.5 * middle / second
        p1, p2, p3 = 1.0 - 2.0 * r, r * r - 2.0 * r, r * r
        coefs = (-r - q * p1, q * (r * p1 - p2), q * (r * p2 - p3), q * r * p3)
        both = first * second
        return both, coefs, scale * both * both

    def transform(places, pack_at=None):
        pack = pack_at is not None
        group = range(len(places))
        xs, sides, scalars = [], [], []
        for i, j in places:
            gram, side = gram_of(i, j)
            ridge = members - 1.0
            trace = total(gram * eye)
            frob = jnp.sqrt(total(gram * gram) + 2.0 * ridge * trace + ridge * ridge * members)
            centre = ridge + trace * (1.0 / members)
            inv = 1.0 / centre
            xs.append(gram * inv + eye * (ridge * inv - 1.0))
            sides.append(side)
            scale = centre / frob
            root, steps = 1.0, []
            for _ in range(ITERS // 2):
                both, coefs, scale = pair_factor(scale)
                root = root * both
                steps.append(coefs)
            scalars.append((frob, root, steps))
        zs = [None for _ in group]
        for step in range(ITERS // 2):
            last = step == ITERS // 2 - 1
            squares, ds, gs = [], [], []
            for x in xs:
                xb = x.astype(BF16)
                squares.append(nn(xb, xb))
            for n in group:
                a1, a2, a3, a4 = scalars[n][2][step]
                x, s = xs[n], squares[n]
                tail = nn(s.astype(BF16), (a3 * x + a4 * s).astype(BF16))
                ds.append(a1 * x + a2 * s + tail)
            for n in group:
                d = ds[n]
                db = d.astype(BF16)
                if not last:
                    gs.append((xs[n] + d) + nn(db, xs[n].astype(BF16)))
                zs[n] = d if step == 0 else (zs[n] + d) + nn(db, zs[n].astype(BF16))
            if not last:
                xs = [(gs[n] + ds[n]) + nn(ds[n].astype(BF16), gs[n].astype(BF16)) for n in group]
        for n, (i, j) in enumerate(places):
            frob, root, _ = scalars[n]
            zb = zs[n].astype(BF16)
            inner = sides[n] + through(sides[n], zb)
            inner = inner * (root * root / frob)
            mean_weight = inner + through(inner, zb)
            spread = math.sqrt(members - 1) * root / jnp.sqrt(frob)
            part = spread * (zs[n] + eye)
            wbuf[i + 1, j + 1] = (part + column(mean_weight)).astype(BF16)
            if pack:
                half = members // 2
                swapped = jnp.concatenate([part[half:, half:], part[half:, :half]], axis=1)
                wpack[pack_at(n)[0], pack_at(n)[1], pl.ds(0, half), :] = jnp.where(
                    upper, part[:half], swapped
                ).astype(BF16)
                diagonal = jnp.sum(part * eye, axis=0, keepdims=True)
                high = mean_weight.astype(BF16).astype(F32)
                wpack[pack_at(n)[0], pack_at(n)[1], pl.ds(half, SIDE_ROWS), :] = jnp.where(
                    which == 0, diagonal,
                    jnp.where(which == 1, high, jnp.where(which == 2, mean_weight - high, 0.0)),
                ).astype(BF16)

    def unpack(side, spot, j):
        half = members // 2
        sent = whalo[side, spot, pl.ds(0, half), :]
        tail = whalo[side, spot, pl.ds(half, SIDE_ROWS), :].astype(F32)
        turned = jnp.transpose(jnp.concatenate([sent, sent], axis=0)).astype(F32)
        sent = sent.astype(F32)
        swapped = jnp.concatenate([sent[:, half:], sent[:, :half]], axis=1)
        top = jnp.where(upper, sent, turned[:half])
        low = jnp.where(lane >= half, jnp.where(lane - half < line, swapped, turned[:half]), turned[half:])
        low = jnp.where(lane - half == line, tail[0:1], low)
        whole = jnp.concatenate([top, low], axis=0) + column(tail[1:2] + tail[2:3])
        wbuf[side * (tile_lat + 1), j] = whole.astype(BF16)

    mid_lat, mid_lon = tile_lat - 2, tile_lon - 2
    n_rows, n_sides, n_inner = 2 * tile_lon, 2 * mid_lat, mid_lat * mid_lon
    group = next(g for g in (4, 2) if all(n % g == 0 for n in (n_rows, n_sides, n_inner)))
    g_rows, g_sides, g_inner = n_rows // group, n_sides // group, n_inner // group
    wide = next(g for g in range(16, 0, -1) if mid_lat * tile_lon % g == 0)
    w_rest = mid_lat * tile_lon // wide
    ready = next(g for g in range(8, 0, -1) if mid_lat * tile_lon % g == 0)

    def row_place(k):
        return (k % 2) * (tile_lat - 1), k // 2

    def side_place(k):
        return 1 + k // 2, (k % 2) * (tile_lon - 1)

    def inner_place(k):
        return 1 + k // mid_lon, 1 + k % mid_lon

    for n in (10, 3, 4, 5, 0, 1):
        loads[n].wait()

    def first_step(t, carry):
        for g in range(2 * part_lon):
            prepare((g % 2) * (tile_lat - 1), t * part_lon + g // 2)

        @pl.when(t == 0)
        def _():
            pl.semaphore_wait(barrier, present)

        for index in range(2):
            where_exists(WAYS[index], lambda index=index: q_row(index, t).start())
        return carry

    lax.fori_loop(0, row_parts, first_step, 0)
    loads[2].wait()

    def ready_step(t, carry):
        for g in range(ready):
            k = t * ready + g
            p = k // mid_lat
            prepare(1 + k % mid_lat, jnp.where(p % 2 == 0, p // 2, tile_lon - 1 - p // 2))

        @pl.when(t == (2 * mid_lat + ready - 1) // ready - 1)
        def _():
            for index in range(2):
                q_lon(index).start()

        return carry

    lax.fori_loop(0, mid_lat * tile_lon // ready, ready_step, 0)
    for index in range(2):
        q_lon(index).wait_recv()

    def rest_step(slot, carry):
        ks = [slot * wide + g for g in range(wide)]
        transform([(1 + k // tile_lon, k % tile_lon) for k in ks])
        return carry

    lax.fori_loop(0, w_rest, rest_step, 0)
    for index in range(2):
        w_copy(index, 0).start()
    for index in range(2):
        for part in range(row_parts):
            received(index, lambda index, part=part: q_row(index, part))
    each_corner(0, lambda copy: copy.start())

    def row_step(part, carry):
        @pl.when(part == row_parts - 1)
        def _():
            each_corner(0, lambda copy: copy.wait_recv())

        spots = [(g % 2, g // 2) for g in range(2 * part_lon)]
        transform(
            [(side * (tile_lat - 1), column_of(part, t)) for side, t in spots],
            lambda n: (spots[n][0], part * part_lon + spots[n][1]),
        )
        for index in range(2):
            where_exists(WAYS[index], lambda index=index: row_copy(index, part).start())
        return carry

    lax.fori_loop(0, row_parts, row_step, 0)
    for index in range(2):
        for part in range(1, 3):
            w_copy(index, part).start()

    def analyse(i, j, side=None):
        values = state_ref[i, j]
        mean = nn(values, flat)
        values = values.astype(F32)
        pert = (values - mean).astype(BF16)
        corner = quadrant_ref[i, pl.ds(j, 1), :]
        kept = land_ref[i, pl.ds(j, 1), :] != 1
        along = []
        for half, frac in (
            (corner // 2, frac_lat_ref[i, pl.ds(j, 1), :]),
            (corner % 2, frac_lon_ref[i, pl.ds(j, 1), :]),
        ):
            along.append(jnp.where(half == 0, 1.0 - frac, 0.0))
            along.append(jnp.where(half == 1, frac, 0.0))
        along[0] = jnp.where(kept, 2.0, along[0])
        along += [jnp.zeros_like(along[1])] * 4
        coef = jnp.transpose(jnp.concatenate(along, axis=0))
        edges = [jnp.broadcast_to(coef[:, n : n + 1], (cells, members)) for n in range(4)]
        kept = edges[0] > 1.5
        spread_lat = (edges[0], 1.0 - edges[0] - edges[1], edges[1])
        spread_lon = (edges[2], 1.0 - edges[2] - edges[3], edges[3])
        halo = None if side is None else 2 * side
        acc = mean
        for a in range(3):
            if a == halo:
                continue
            wide = jnp.concatenate([wbuf[i + a, j + b] for b in range(3)], axis=1)
            prod = nn(pert, wide)
            row = sum(
                spread_lon[b] * prod[:, b * members : (b + 1) * members] for b in range(3)
            )
            acc = acc + spread_lat[a] * row
        acc = jnp.where(kept, values, acc)
        if side is None:
            out_ref[i, j] = acc.astype(BF16)
        else:
            share = jnp.where(kept, 0.0, spread_lat[halo])
            acc_ref[side, j] = acc
            pert_ref[side, j] = pert
            for b in range(3):
                share_ref[side, j, b] = share * spread_lon[b]

    def finish(side, j):
        i = side * (tile_lat - 1)
        wide = jnp.concatenate([wbuf[side * (tile_lat + 1), j + b] for b in range(3)], axis=1)
        prod = nn(pert_ref[side, j], wide)
        acc = acc_ref[side, j]
        for b in range(3):
            acc = acc + share_ref[side, j, b] * prod[:, b * members : (b + 1) * members]
        out_ref[i, j] = acc.astype(BF16)

    for n in range(6, 10):
        loads[n].wait()
    def analyse_all(count, place):
        each = next(g for g in range(12, 0, -1) if count % g == 0)

        def step(t, carry):
            for g in range(each):
                analyse(*place(t * each + g))
            return carry

        lax.fori_loop(0, count // each, step, 0)

    analyse_all(n_inner, inner_place)
    for index in range(2):
        for part in range(3):
            w_copy(index, part).wait_recv()
    each_own = next(g for g in (4, 2, 1) if tile_lon % g == 0)

    def own_step(t, carry):
        for g in range(each_own):
            for side in range(2):
                analyse(side * (tile_lat - 1), t * each_own + g, side)
        return carry

    lax.fori_loop(0, tile_lon // each_own, own_step, 0)

    def unpack_step(part, carry):
        for index in range(2):
            received(index, lambda index: row_copy(index, part))

        @pl.when(part == row_parts - 1)
        def _():
            each_corner(1, lambda copy: copy.start())

        for t in range(part_lon):
            for side in range(2):
                unpack(side, part * part_lon + t, 1 + column_of(part, t))
        return carry

    lax.fori_loop(0, row_parts, unpack_step, 0)
    analyse_all(n_sides, side_place)
    for j in range(1, tile_lon - 1):
        for side in range(2):
            finish(side, j)
    each_corner(1, lambda copy: copy.wait_recv())
    for side in range(2):
        for n in range(2):
            unpack(side, tile_lon + n, n * (tile_lon + 1))
    for j in (0, tile_lon - 1):
        for side in range(2):
            finish(side, j)
    for index in range(2):
        q_lon(index).wait_send()
        for part in range(3):
            w_copy(index, part).wait_send()
        for part in range(row_parts):
            sent(index, lambda index, part=part: q_row(index, part))
            sent(index, lambda index, part=part: row_copy(index, part))
    each_corner(0, lambda copy: copy.wait_send())
    each_corner(1, lambda copy: copy.wait_send())


ANY = pl.BlockSpec(memory_space=pltpu.HBM)


def body(counts, state, obs_row, obs_count, obs_value, obs_weight, quadrant, frac_lat, frac_lon, land):
    tile_lat, tile_lon, cells, members = state.shape
    rows = cells + SIDE_ROWS
    row_parts = 2 if tile_lon % 4 == 0 else 1
    packed = members // 2 + SIDE_ROWS
    hbm = pltpu.HBM
    arrays = (state, obs_row, obs_value, obs_weight, quadrant, frac_lat, frac_lon, land)
    dma = pltpu.SemaphoreType.DMA
    return pl.pallas_call(
        functools.partial(main_kernel, counts),
        out_shape=jax.ShapeDtypeStruct(state.shape, BF16),
        in_specs=[ANY] * (1 + len(arrays)),
        out_specs=pl.BlockSpec(memory_space=pltpu.VMEM),
        scratch_shapes=[pltpu.SMEM(obs_count.shape, obs_count.dtype)]
        + [pltpu.VMEM(x.shape, x.dtype) for x in arrays]
        + [
            pltpu.VMEM((2, tile_lon, cells, members), F32),
            pltpu.VMEM((2, tile_lon, 3, cells, members), F32),
            pltpu.VMEM((2, tile_lon, cells, members), BF16),
            pltpu.VMEM((tile_lat + 2, tile_lon + 2, rows, members), BF16),
            pltpu.VMEM((tile_lat + 2, tile_lon + 2, members, members), BF16),
            pltpu.VMEM((2, tile_lon, packed, members), BF16),
            pltpu.VMEM((2, tile_lon + 2, packed, members), BF16),
            dma((11,)),
            dma((2,)),
            dma((2,)),
            dma((2, 3)),
            dma((2, 3)),
            dma((2, 2, row_parts)),
            dma((2, 2, row_parts)),
            dma((2, 4)),
            dma((2, 4)),
        ],
        compiler_params=pltpu.CompilerParams(
            collective_id=0, has_side_effects=True, vmem_limit_bytes=48 * 1024 * 1024
        ),
        name="analyse",
    )(*(pltpu.with_memory_space_constraint(x, hbm) for x in (obs_count, *arrays)))


def solution(mesh):
    counts = (mesh.shape["lat"], mesh.shape["lon"])
    return jax.shard_map(
        functools.partial(body, counts),
        mesh=mesh,
        in_specs=(
            P("lat", "lon", None, None),
            P("lat", "lon", None),
            P("lat", "lon"),
            P("lat", "lon", None),
            P("lat", "lon", None),
            P("lat", "lon", None),
            P("lat", "lon", None),
            P("lat", "lon", None),
            P("lat", "lon", None),
        ),
        out_specs=P("lat", "lon", None, None),
        check_vma=False,
    )
```
